32 devices in a mesh: gx: 8 (over z, x), yz: 4 (over y, core).
Axes of the slice: x: 2, y: 2, z: 4, core: 2. Of those that a mesh axis runs over, the one named last changes fastest.
Arguments:
- velocity: bfloat16 [3, 8, 1024, 2048], P(None, 'gx', None, 'yz'), may hold values from -6 to 6
- mean_flow: float32 [1024], replicated, may hold values from 0.5 to 1.5
- chol_diag: float32 [3, 1024], replicated, may hold values from 0.3 to 3
- chol_off: float32 [3, 1024], replicated, may hold values from -3 to 3
- eddy_x: int32 [1536], replicated, may hold values from -64 to 63
- eddy_y: int32 [1536], replicated, may hold values from 0 to 1023
- eddy_z: int32 [1536], replicated, may hold values from 0 to 2047, as said below
- eddy_signs: int32 [3, 1536], replicated, may hold values from 0 to 1
- tile_lists: int32 [16, 288], P('yz'), may hold values from 0 to 1535, as said below
Outputs:
- velocity_next: bfloat16 [3, 8, 1024, 2048], P(None, 'gx', None, 'yz')
- inflow: float32 [1, 3, 1024, 2048], P(None, None, None, 'yz')
The draws below stay inside these ranges and needn't reach their ends.
Inputs may be any that keep to these rules, and one draw needn't show every extreme that they name: Each tile of 128 spanwise cells is the home of exactly 96 eddies; the home tile of eddy e is eddy_z[e] // 128. `tile_lists`: row t holds, in some order and each once, exactly the eddies whose home tile is t - 1, t or t + 1, counted modulo 16.
All inputs are finite; a program needn't handle non-finite values.
Results may differ from the reference program's by a relative error of at most 0.0047.
Values may be sent and summed in bfloat16 or wider, within the bound.
A program may use at most 192 MiB of HBM per device.

```python
import math
import jax
import jax.numpy as jnp
from jax import lax

NS = 2048
NW = 1024
TILE = 128
STEPS = 1
EPT = 96
SIGMA = 64
TILES = 16
EDDIES = 1536
NX = 8


def eddy_layout(key):
    base = jax.random.fold_in(key, 11)
    key_order, key_offset, key_rows = jax.random.split(base, 3)
    order = jax.random.permutation(key_order, EDDIES).astype(jnp.int32)
    slots = jnp.arange(EDDIES, dtype=jnp.int32)
    home = slots // EPT
    offset = jax.random.randint(key_offset, (EDDIES,), 0, TILE, dtype=jnp.int32)
    centres = jnp.zeros((EDDIES,), jnp.int32).at[order].set(home * TILE + offset)
    tiles = jnp.arange(TILES, dtype=jnp.int32)
    nearby = jnp.stack([(tiles - 1) % TILES, tiles, (tiles + 1) % TILES], axis=1)
    slot_rows = (nearby[:, :, None] * EPT + jnp.arange(EPT, dtype=jnp.int32)[None, None, :]).reshape(TILES, 3 * EPT)
    members = order[slot_rows]
    row_keys = jax.random.split(key_rows, TILES)

    def shuffle_row(row_key, row_values):
        return jax.random.permutation(row_key, row_values)
    shuffled = jax.vmap(shuffle_row)(row_keys, members)
    return (centres, shuffled.astype(jnp.int32))


def draw_eddy_z(key, part):
    centres, listed = eddy_layout(key)
    return centres


def draw_tile_lists(key, part):
    centres, listed = eddy_layout(key)
    return listed


def place_ends(values, rng, low, high):
    shape = values.shape
    index_at = [jax.random.randint(jax.random.fold_in(rng, axis), (), 0, shape[axis]) for axis in range(len(shape))]
    values = values.at[tuple(index_at)].set(low)
    longest = shape.index(max(shape))
    index_at[longest] = (index_at[longest] + 1) % shape[longest]
    return values.at[tuple(index_at)].set(high)


def block_levels(rng, extent, cuts, smallest, top_value):
    gain = 1.0
    for position, blocks in cuts:
        heights = jax.random.uniform(jax.random.fold_in(jax.random.fold_in(rng, 6), position), (blocks,), jnp.float32, smallest / len(cuts), top_value / len(cuts))
        gain = gain * jnp.repeat(jnp.exp(heights), extent[position] // blocks).reshape((-1,) + (1,) * (len(extent) - 1 - position))
    return gain


def noise(rng, extent, deviation, most, cuts=(), held_as=jnp.bfloat16):
    gain = block_levels(rng, extent, cuts, -0.22, 0.18) if cuts else 1.0
    drawn = jax.random.normal(rng, extent, jnp.float32) * deviation * gain
    return jnp.minimum(jnp.maximum(drawn, -most), most).astype(held_as)


def setup_inputs(seed: int = 0) -> dict:
    splits = jax.random.split(jax.random.key(seed), 10)
    return {
        "velocity": noise(splits[0], (3, NX, NW, NS), 1.0, 6.0, ((1, 8), (3, 4))),
        "mean_flow": jnp.clip(jax.random.uniform(splits[1], (NW,), jnp.float32, 0.5, 1.5), 0.5, 1.5),
        "chol_diag": jnp.clip(jnp.exp(jax.random.uniform(splits[2], (3, NW), jnp.float32, math.log(0.3), math.log(3.0))), 0.3, 3.0),
        "chol_off": noise(splits[3], (3, NW), 0.5, 3.0, (), jnp.float32),
        "eddy_x": place_ends(jax.random.randint(splits[4], (EDDIES,), -SIGMA, SIGMA), jax.random.fold_in(splits[4], 1), -SIGMA, SIGMA - 1).astype(jnp.int32),
        "eddy_y": place_ends(jax.random.randint(splits[5], (EDDIES,), 0, NW), jax.random.fold_in(splits[5], 1), 0, NW - 1).astype(jnp.int32),
        "eddy_z": draw_eddy_z(jax.random.fold_in(splits[9], 71), 0),
        "eddy_signs": place_ends(jax.random.randint(splits[7], (3, EDDIES), 0, 2), jax.random.fold_in(splits[7], 1), 0, 1).astype(jnp.int32),
        "tile_lists": draw_tile_lists(jax.random.fold_in(splits[9], 71), 0),
    }


shape_peak = math.sqrt(1.5)
time_step = 0.4
viscosity = 0.3
bulk_speed = 1.0

def tent_shape(ratio):
    return shape_peak * jnp.maximum(0.0, 1.0 - jnp.abs(ratio))

def section_offsets():
    offsets = [float(step_index) for step_index in range(STEPS)]
    return jnp.array(offsets, dtype=jnp.float32) * (bulk_speed * time_step)

def tile_weights(listed_row, tile_index, eddy_x, eddy_y, eddy_z, sign_values, offsets):
    cells_y = jnp.arange(NW, dtype=jnp.int32)
    shape_y = tent_shape((cells_y[None, :] - eddy_y[listed_row][:, None]).astype(jnp.float32) / SIGMA)
    cells_z = tile_index * TILE + jnp.arange(TILE, dtype=jnp.int32)
    offset_z = (cells_z[None, :] - eddy_z[listed_row][:, None] + NS // 2) % NS - NS // 2
    shape_z = tent_shape(offset_z.astype(jnp.float32) / SIGMA)
    shape_x = tent_shape((eddy_x[listed_row].astype(jnp.float32)[None, :] + offsets[:, None]) / SIGMA)
    amplitude = math.sqrt(8.0 * NW / (TILE * EPT))
    weights = amplitude * shape_x[:, None, :, None] * sign_values[:, listed_row][None, :, :, None] * shape_z[None, None]
    return (shape_y.astype(jnp.bfloat16), weights.astype(jnp.bfloat16))

def cosine_basis():
    mode_index = jnp.arange(NW, dtype=jnp.int32)[:, None]
    cell_index = jnp.arange(NW, dtype=jnp.int32)[None, :]
    angles = (mode_index * (2 * cell_index + 1) % (4 * NW)).astype(jnp.float32) * (math.pi / (2 * NW))
    norms = jnp.where(mode_index == 0, math.sqrt(1.0 / NW), math.sqrt(2.0 / NW))
    return norms * jnp.cos(angles)

def cholesky_inlet(fluct, mean_flow, chol_diag, chol_off):
    first = mean_flow[:, None] + chol_diag[0][:, None] * fluct[:, 0]
    second = chol_off[0][:, None] * fluct[:, 0] + chol_diag[1][:, None] * fluct[:, 1]
    third = chol_off[1][:, None] * fluct[:, 0] + chol_off[2][:, None] * fluct[:, 1] + chol_diag[2][:, None] * fluct[:, 2]
    return (first, second, third)

def wall_flux(second):
    keep = (jnp.arange(NW, dtype=jnp.int32) < NW - 1).astype(jnp.float32)[:, None]
    return second * keep

def eigen_scale(mode_y, mode_z):
    rise_y = 2.0 - 2.0 * jnp.cos(mode_y.astype(jnp.float32) * (math.pi / NW))
    rise_z = 2.0 - 2.0 * jnp.cos(mode_z.astype(jnp.float32) * (2.0 * math.pi / NS))
    eigen_sum = -(rise_y + rise_z)
    mean_mode = (mode_y == 0) & (mode_z == 0)
    return jnp.where(mean_mode, 0.0, 1.0 / jnp.where(mean_mode, -1.0, eigen_sum))

def tendency(field, inlet_plane, mean_flow):
    behind = jnp.concatenate([inlet_plane[:, None], field[:, :-1]], axis=1)
    behind = lax.optimization_barrier(behind.astype(jnp.bfloat16)).astype(jnp.float32)
    edge = jnp.zeros_like(field[:, :, :1])
    above = jnp.concatenate([field[:, :, 1:], edge], axis=2)
    below = jnp.concatenate([edge, field[:, :, :-1]], axis=2)
    return -mean_flow[:, None] * (field - behind) - 0.5 * field[1] * (above - below) + viscosity * (above - 2.0 * field + below)

def march(field, inflow, mean_flow):
    for step_index in range(STEPS):
        plane = inflow[step_index]
        first_rate = tendency(field, plane, mean_flow)
        section_one = field + time_step * (8.0 / 15.0) * first_rate
        second_rate = tendency(section_one, plane, mean_flow)
        section_two = section_one + time_step * (5.0 / 12.0 * second_rate - 17.0 / 60.0 * first_rate)
        third_rate = tendency(section_two, plane, mean_flow)
        field = section_two + time_step * (0.75 * third_rate - 5.0 / 12.0 * second_rate)
    return field

def reference(velocity, mean_flow, chol_diag, chol_off, eddy_x, eddy_y, eddy_z, eddy_signs, tile_lists):
    offsets = section_offsets()
    sign_values = (2 * eddy_signs - 1).astype(jnp.float32)

    def one_tile(packed):
        listed_row, tile_index = packed
        shape_y, weights = tile_weights(listed_row, tile_index, eddy_x, eddy_y, eddy_z, sign_values, offsets)
        return jnp.einsum('ly,njlz->njyz', shape_y.astype(jnp.float32), weights.astype(jnp.float32))
    per_tile = lax.map(one_tile, (tile_lists, jnp.arange(TILES, dtype=jnp.int32)))
    fluct = jnp.moveaxis(per_tile, 0, 3).reshape(STEPS, 3, NW, NS)
    first, second, third = cholesky_inlet(fluct, mean_flow, chol_diag, chol_off)
    basis = cosine_basis()
    flux = wall_flux(second)
    lower = jnp.concatenate([jnp.zeros_like(flux[:, :1]), flux[:, :-1]], axis=1)
    div = flux - lower + third - jnp.roll(third, 1, axis=2)
    high = lax.Precision.HIGHEST
    div_modes = jnp.einsum('ky,nyz->nkz', basis, div, precision=high)
    spectrum = jnp.fft.fft(div_modes, axis=2)
    scale = eigen_scale(jnp.arange(NW, dtype=jnp.int32)[:, None], jnp.arange(NS, dtype=jnp.int32)[None, :])
    potential_modes = jnp.real(jnp.fft.ifft(spectrum * scale, axis=2)).astype(jnp.float32)
    potential = jnp.einsum('ky,nkz->nyz', basis, potential_modes, precision=high)
    slope_z = jnp.roll(potential, -1, axis=2) - potential
    rise = jnp.concatenate([potential[:, 1:] - potential[:, :-1], jnp.zeros_like(potential[:, :1])], axis=1)
    inflow = jnp.stack([first, flux - rise, third - slope_z], axis=1)

    def one_block(tile_index):
        start = (tile_index * TILE).astype(jnp.int32)
        block = lax.dynamic_slice_in_dim(velocity, start, TILE, 3).astype(jnp.float32)
        plane = lax.dynamic_slice_in_dim(inflow, start, TILE, 3)
        return march(block, plane, mean_flow).astype(jnp.bfloat16)
    marched = lax.map(one_block, jnp.arange(TILES, dtype=jnp.int32))
    velocity_next = marched.transpose(1, 2, 3, 0, 4).reshape(3, NX, NW, NS)
    return (velocity_next, inflow)
```

```python
import functools
import math

import jax
import jax.numpy as jnp
import numpy as np
from jax import lax
from jax.experimental import pallas as pl
from jax.experimental.pallas import tpu as pltpu
from jax.sharding import PartitionSpec as P

TILE = 128
EPT = 96
SIGMA = 64
LANES = 128
STRIDE = 128
HALO = 16
WINDOW = STRIDE + 2 * HALO
BAND = 256
MESH = pl.DeviceIdType.MESH

shape_peak = math.sqrt(1.5)
time_step = 0.4
viscosity = 0.3

THETA, RATE, RATE2, RATE4, ALPHA, BETA, PERIOD, POWERS = range(8)


def tent_shape(ratio):
    return shape_peak * jnp.maximum(0.0, 1.0 - jnp.abs(ratio))


def wall_bases(rows):
    k = np.arange(rows)[None, :]
    y = np.arange(rows)[:, None]
    norm = np.where(k == 0, math.sqrt(1.0 / rows), math.sqrt(2.0 / rows))
    cosine = norm * np.cos((k * (2 * y + 1) % (4 * rows)) * (math.pi / (2 * rows)))
    sine = math.sqrt(2.0 / rows) * np.sin((k * (y + 1) % (2 * rows)) * (math.pi / rows))
    high = cosine.astype(jnp.bfloat16)
    low = (cosine - high.astype(np.float64)).astype(jnp.bfloat16)
    return high, low, sine.astype(jnp.bfloat16)


def mode_table(rows, length, count):
    theta = 2.0 * np.arcsinh(np.sin(np.arange(rows) * (math.pi / (2 * rows))))
    rate = np.exp(-theta)
    period = np.where(theta > 0, 1.0 / np.maximum(-np.expm1(-theta * length * count), 1e-30), 1.0)
    table = [theta, rate, rate**2, rate**4, rate / (1.0 + rate), np.sqrt(rate) / (1.0 + rate), period]
    table += [np.exp(-theta * length * q) for q in range(count)]
    table += [np.zeros(rows)] * (-len(table) % 8)
    return np.stack(table).astype(np.float32)


def dot(a, b, contract):
    return lax.dot_general(a, b, (contract, ((), ())), preferred_element_type=jnp.float32)


NN = ((1,), (0,))
NT = ((1,), (1,))


def step_kernel(
    slabs, count,
    vel_ref, cos_hbm, low_hbm, sin_hbm, mean_ref, diag_ref, off_ref, x_ref, y_ref, z_ref, sign_ref, table_ref,
    next_ref, flow_ref,
    keep, other, near, further, far, back,
    cosine, cosine_low, sine, params, weight, edge_weight, carry_row,
    div_high, div_low, modes, ups, downs, slope_modes, rise_modes, sums,
    load_sem, other_send, other_recv, near_send, near_recv, further_send, further_recv,
    far_send, far_recv, back_send, back_recv, sum_send, sum_recv,
):
    rows, columns = flow_ref.shape[1:]
    half = columns // 2
    spanwise = columns * count
    eddies = x_ref.shape[1]
    blocks = rows // STRIDE
    me = lax.axis_index("gx")
    pencil = lax.axis_index("yz")
    parity = lax.rem(me, 2)
    even = parity == 0
    partner = me + 1 - 2 * parity
    has_after = me + 2 < slabs
    has_before = me >= 2
    gets_far = me >= 4
    gives_far = has_after & (me >= 2)
    after = jnp.where(has_after, me + 2, me - 2)
    at_inlet = me < 2
    after_inlet = (me >= 2) & (me < 4)
    mine_at = pl.multiple_of(parity * half, half)
    theirs_at = pl.multiple_of((1 - parity) * half, half)

    barrier = pltpu.get_barrier_semaphore()
    pl.semaphore_signal(barrier, inc=1, device_id={"gx": partner}, device_id_type=MESH)
    for step in range(1, count):
        pl.semaphore_signal(barrier, inc=1, device_id={"yz": lax.rem(pencil + step, count)}, device_id_type=MESH)

    @pl.when(has_after)
    def _():
        pl.semaphore_signal(barrier, inc=1, device_id={"gx": after}, device_id_type=MESH)

    @pl.when(has_before)
    def _():
        pl.semaphore_signal(barrier, inc=1, device_id={"gx": me - 2}, device_id_type=MESH)

    loads = [
        pltpu.make_async_copy(vel_ref.at[:, :, pl.ds(mine_at, half)], keep, load_sem.at[0]),
        pltpu.make_async_copy(cos_hbm, cosine, load_sem.at[1]),
        pltpu.make_async_copy(low_hbm, cosine_low, load_sem.at[2]),
        pltpu.make_async_copy(sin_hbm, sine, load_sem.at[3]),
    ]
    for load in loads:
        load.start()

    pl.semaphore_wait(barrier, count + has_after.astype(jnp.int32) + has_before.astype(jnp.int32))

    def block_rows(block):
        return pl.ds(pl.multiple_of(block * STRIDE, STRIDE), STRIDE)

    def send(source, target, block, send_sem, recv_sem, device):
        return pltpu.make_async_remote_copy(
            src_ref=source,
            dst_ref=target,
            send_sem=send_sem.at[block],
            recv_sem=recv_sem.at[block],
            device_id={"gx": device},
            device_id_type=MESH,
        )

    def other_copy(block):
        here = block_rows(block)
        return send(
            vel_ref.at[:, here, pl.ds(theirs_at, half)], other.at[:, here, :], block, other_send, other_recv, partner
        )

    def near_copy(block):
        here = block_rows(block)
        return send(vel_ref.at[:, here, pl.ds(mine_at, half)], near.at[:, here, :], block, near_send, near_recv, after)

    def further_copy(block):
        here = block_rows(block)
        return send(other.at[:, here, :], further.at[:, here, :], block, further_send, further_recv, after)

    def far_copy(source, block):
        here = block_rows(block)
        return send(source.at[:, here, :], far.at[:, here, :], block, far_send, far_recv, after)

    def back_copy(block):
        here = block_rows(block)
        return send(
            back.at[:, here, :], next_ref.at[:, here, pl.ds(mine_at, half)], block, back_send, back_recv, partner
        )

    @pl.loop(0, blocks)
    def _(block):
        other_copy(block).start()

        @pl.when(has_after)
        def _():
            near_copy(block).start()

    def start_further(block):
        other_copy(block).wait_recv()

        @pl.when(has_after)
        def _():
            further_copy(block).start()

    def start_far(block):
        @pl.when(has_before)
        def _():
            near_copy(block).wait_recv()
            further_copy(block).wait_recv()

        @pl.when(gives_far & even)
        def _():
            far_copy(further, block).start()

        @pl.when(gives_far & (parity == 1))
        def _():
            far_copy(near, block).start()

    @pl.when(at_inlet)
    def _():
        near[...] = jnp.zeros_like(near)
        further[...] = jnp.zeros_like(further)

    @pl.when(me < 4)
    def _():
        far[...] = jnp.zeros_like(far)

    for place, row in enumerate(
        [mean_ref[0:1, :]] + [diag_ref[c : c + 1, :] for c in range(3)] + [off_ref[c : c + 1, :] for c in range(3)]
    ):
        params[place] = jnp.transpose(jnp.broadcast_to(row, (LANES, rows)))

    first_cell = pencil * columns
    amplitude = math.sqrt(8.0 * rows / (TILE * EPT))
    stretch = amplitude * tent_shape(x_ref[...].astype(jnp.float32) / SIGMA)
    scales = [stretch * (2 * sign_ref[j : j + 1, :] - 1).astype(jnp.float32) for j in range(3)]

    def weights(start, extent):
        cells = start + lax.broadcasted_iota(jnp.int32, (extent, eddies), 0)
        offset = cells - z_ref[...]
        offset = jnp.where(offset >= spanwise // 2, offset - spanwise, offset)
        offset = jnp.where(offset < -(spanwise // 2), offset + spanwise, offset)
        shape_z = tent_shape(offset.astype(jnp.float32) / SIGMA)
        return [(scale * shape_z).astype(jnp.bfloat16) for scale in scales]

    @pl.loop(0, columns // LANES)
    def _(tile):
        start = pl.multiple_of(tile * LANES, LANES)
        for j, value in enumerate(weights(first_cell + start, LANES)):
            weight[j, pl.ds(start, LANES), :] = value

    for j, value in enumerate(weights(jnp.where(pencil == 0, spanwise, first_cell) - 1, 16)):
        edge_weight[j] = value

    carry_row[...] = jnp.zeros_like(carry_row)

    @pl.loop(0, rows // BAND)
    def _(band):
        start = pl.multiple_of(band * BAND, BAND)
        here = pl.ds(start, BAND)
        cells = start + lax.broadcasted_iota(jnp.int32, (BAND, eddies), 0)
        shape_y = tent_shape((cells - y_ref[...]).astype(jnp.float32) / SIGMA).astype(jnp.bfloat16)
        fl = [dot(shape_y, weight[j], NT) for j in range(3)]
        ends = [dot(shape_y, edge_weight[j], NT)[:, 0:1] for j in range(3)]

        def spread(place):
            return jnp.concatenate([params[place, here, :]] * (columns // LANES), axis=1)

        flow_ref[0, here, :] = spread(0) + spread(1) * fl[0]
        row = start + lax.broadcasted_iota(jnp.int32, (BAND, columns), 0)
        flux = jnp.where(row == rows - 1, 0.0, spread(4) * fl[0] + spread(2) * fl[1])
        third = spread(5) * fl[0] + spread(6) * fl[1] + spread(3) * fl[2]
        edge = (
            params[5, here, 0:1] * ends[0] + params[6, here, 0:1] * ends[1] + params[3, here, 0:1] * ends[2]
        )
        lower = jnp.where(row == start, carry_row[0:1, :], pltpu.roll(flux, 1, 0))
        lane = lax.broadcasted_iota(jnp.int32, (BAND, columns), 1)
        previous = jnp.where(lane == 0, edge, pltpu.roll(third, 1, 1))
        carry_row[0:1, :] = flux[BAND - 1 : BAND, :]
        flow_ref[1, here, :] = flux
        flow_ref[2, here, :] = third
        div = jnp.transpose(flux - lower + third - previous)
        high = div.astype(jnp.bfloat16)
        div_high[:, here] = high
        div_low[:, here] = (div - high.astype(jnp.float32)).astype(jnp.bfloat16)

    loads[1].wait()
    loads[2].wait()

    @pl.loop(0, rows // BAND)
    def _(band):
        here = pl.ds(pl.multiple_of(band * BAND, BAND), BAND)
        wall = cosine[:, here]
        modes[:, here] = (
            dot(div_high[...], wall, NN) + dot(div_low[...], wall, NN) + dot(div_high[...], cosine_low[:, here], NN)
        )

    def entry(place):
        return table_ref[place : place + 1, :]

    line = lax.broadcasted_iota(jnp.int32, (8, rows), 0)
    line_f = line.astype(jnp.float32)
    theta, rate, rate2, rate4 = entry(THETA), entry(RATE), entry(RATE2), entry(RATE4)
    steps = columns // 8

    def scan_step(step, carry):
        up_carry, down_carry, run = carry
        at = pl.ds(pl.multiple_of(step * 8, 8), 8)
        value = modes[at, :]
        value = value + jnp.where(line >= 1, rate, 0.0) * pltpu.roll(value, 1, 0)
        value = value + jnp.where(line >= 2, rate2, 0.0) * pltpu.roll(value, 2, 0)
        value = value + jnp.where(line >= 4, rate4, 0.0) * pltpu.roll(value, 4, 0)
        value = value + jnp.exp(-theta * (line_f + 1.0)) * up_carry
        ups[at, :] = value
        at = pl.ds(pl.multiple_of((steps - 1 - step) * 8, 8), 8)
        down = modes[at, :]
        down = down + jnp.where(line < 7, rate, 0.0) * pltpu.roll(down, 7, 0)
        down = down + jnp.where(line < 6, rate2, 0.0) * pltpu.roll(down, 6, 0)
        down = down + jnp.where(line < 4, rate4, 0.0) * pltpu.roll(down, 4, 0)
        down = down + jnp.exp(-theta * (8.0 - line_f)) * down_carry
        downs[at, :] = jnp.where(line == 7, down_carry, pltpu.roll(down, 7, 0))
        return value[7:8, :], down[0:1, :], run + value

    zeros = jnp.zeros((1, rows), jnp.float32)
    sum_up, sum_down, run = lax.fori_loop(0, steps, scan_step, (zeros, zeros, jnp.zeros((8, rows), jnp.float32)))
    run = jnp.sum(run, axis=0, keepdims=True)
    sums[pencil] = jnp.where(line == 0, sum_up, jnp.where(line == 1, sum_down, run))

    def sum_copy(step):
        return pltpu.make_async_remote_copy(
            src_ref=sums.at[pencil],
            dst_ref=sums.at[pencil],
            send_sem=sum_send.at[step - 1],
            recv_sem=sum_recv.at[step - 1],
            device_id={"yz": lax.rem(pencil + step, count)},
            device_id_type=MESH,
        )

    for step in range(1, count):
        sum_copy(step).start()
    for step in range(1, count):
        sum_copy(step).wait_send()
        sum_copy(step).wait_recv()

    total_cells = float(spanwise)
    mean = sum(sums[p, 0:1, :] for p in range(count)) / total_cells
    carry_up, carry_down = zeros, zeros
    start, own, before, shift = zeros, zeros, zeros, zeros
    for p in range(count):
        behind = lax.rem(pencil - 1 - p + 2 * count, count)
        ahead = lax.rem(p - pencil - 1 + count, count)
        carry_up = carry_up + table_ref[pl.ds(POWERS + behind, 1), :] * sums[p, 0:1, :]
        carry_down = carry_down + table_ref[pl.ds(POWERS + ahead, 1), :] * sums[p, 1:2, :]
        total = sums[p, 0:1, :] - mean * columns
        start = start + jnp.where(pencil == p, before, 0.0)
        own = own + jnp.where(pencil == p, total, 0.0)
        shift = shift + sums[p, 2:3, :] - mean * (columns * (columns + 1) / 2.0) + columns * before
        before = before + total
    start = start - shift / total_cells
    first = lax.broadcasted_iota(jnp.int32, (1, rows), 1) == 0
    carry_up = jnp.where(first, start, entry(PERIOD) * carry_up)
    carry_down = jnp.where(first, -start - own, entry(PERIOD) * carry_down)
    mean = jnp.where(first, mean, 0.0)
    alpha, beta = entry(ALPHA), entry(BETA)

    @pl.loop(0, steps // 2)
    def _(step):
        slopes, rises = [], []
        for part in range(2):
            at = pl.ds(pl.multiple_of(step * 16 + part * 8, 8), 8)
            up_count = line_f + (step * 16 + part * 8 + 1).astype(jnp.float32)
            down_count = columns - up_count
            up = ups[at, :] + jnp.exp(-theta * up_count) * carry_up - mean * up_count
            down = downs[at, :] + jnp.exp(-theta * down_count) * carry_down - mean * down_count
            slopes.append(alpha * (up - down))
            rises.append(beta * (up + rate * down))
        at = pl.ds(pl.multiple_of(step * 16, 16), 16)
        slope_modes[at, :] = jnp.concatenate(slopes, axis=0).astype(jnp.bfloat16)
        rise_modes[at, :] = jnp.concatenate(rises, axis=0).astype(jnp.bfloat16)

    lead = min(3, blocks)
    for block in range(lead):
        start_further(block)

    loads[3].wait()

    @pl.loop(0, rows // BAND)
    def _(band):
        here = pl.ds(pl.multiple_of(band * BAND, BAND), BAND)
        flow_ref[2, here, :] = flow_ref[2, here, :] - dot(cosine[here, :], slope_modes[...], NT)
        flow_ref[1, here, :] = flow_ref[1, here, :] - dot(sine[here, :], rise_modes[...], NT)

    loads[0].wait()
    local = lax.broadcasted_iota(jnp.int32, (WINDOW, LANES), 0)

    def march_block(block):
        start = pl.multiple_of(jnp.clip(block * STRIDE - HALO, 0, rows - WINDOW), HALO)
        here = pl.ds(start, WINDOW)

        @pl.loop(0, half // LANES)
        def _(column):
            lanes = pl.ds(pl.multiple_of(column * LANES, LANES), LANES)
            wide = pl.ds(pl.multiple_of(mine_at + column * LANES, LANES), LANES)
            low_wall = local + start == 0
            high_wall = local + start == rows - 1
            mean = params[0, here, :]
            drag = mean + 2.0 * viscosity

            def load(ref):
                return [ref[c, here, lanes].astype(jnp.float32) for c in range(3)]

            def rate(field, behind):
                half_v = 0.5 * field[1]
                up, down = viscosity - half_v, viscosity + half_v
                out = []
                for c in range(3):
                    above = jnp.where(high_wall, 0.0, jnp.roll(field[c], -1, axis=0))
                    below = jnp.where(low_wall, 0.0, jnp.roll(field[c], 1, axis=0))
                    out.append(up * above + down * below + mean * behind[c] - drag * field[c])
                return out

            def pick(flag, first, second):
                return [jnp.where(flag, a, b) for a, b in zip(first, second)]

            def rounded(field):
                return [a.astype(jnp.bfloat16).astype(jnp.float32) for a in field]

            def one(field, f0):
                return [u + time_step * (8.0 / 15.0) * a for u, a in zip(field, f0)]

            def two(field, f1, f0):
                return [
                    u + (time_step * 5.0 / 12.0) * b - (time_step * 17.0 / 60.0) * a
                    for u, b, a in zip(field, f1, f0)
                ]

            def three(field, f2, f1):
                return [
                    u + (time_step * 0.75) * b - (time_step * 5.0 / 12.0) * a
                    for u, b, a in zip(field, f2, f1)
                ]

            inlet = rounded([flow_ref[c, here, wide] for c in range(3)])
            kept, swapped, behind, beyond = load(keep), load(other), load(near), load(further)
            p0, p1 = pick(even, kept, swapped), pick(even, swapped, kept)
            q0, q1 = pick(even, behind, beyond), pick(even, beyond, behind)
            q0_1 = rounded(one(q0, rate(q0, pick(after_inlet, inlet, load(far)))))
            q1_f0 = rate(q1, q0)
            q1_1 = one(q1, q1_f0)
            q1_2 = rounded(two(q1_1, rate(q1_1, q0_1), q1_f0))
            p0_f0 = rate(p0, pick(at_inlet, inlet, q1))
            p0_1 = one(p0, p0_f0)
            p0_f1 = rate(p0_1, pick(at_inlet, inlet, rounded(q1_1)))
            p0_2 = two(p0_1, p0_f1, p0_f0)
            p0_3 = three(p0_2, rate(p0_2, pick(at_inlet, inlet, q1_2)), p0_f1)
            p1_f0 = rate(p1, p0)
            p1_1 = one(p1, p1_f0)
            p1_f1 = rate(p1_1, rounded(p0_1))
            p1_2 = two(p1_1, p1_f1, p1_f0)
            p1_3 = three(p1_2, rate(p1_2, rounded(p0_2)), p1_f1)
            results = ((next_ref, wide, pick(even, p0_3, p1_3)), (back, lanes, pick(even, p1_3, p0_3)))

            def store(skip):
                for ref, at, value in results:
                    for c in range(3):
                        ref[c, block_rows(block), at] = value[c][skip : skip + STRIDE].astype(ref.dtype)

            pl.when(block == 0)(lambda: store(0))
            pl.when((block > 0) & (block < blocks - 1))(lambda: store(HALO))
            pl.when(block == blocks - 1)(lambda: store(2 * HALO))

        back_copy(block).start()

    start_far(0)

    @pl.loop(0, blocks + 1)
    def _(block):
        @pl.when(block + 1 < blocks)
        def _():
            start_far(block + 1)

        @pl.when(block + lead < blocks)
        def _():
            start_further(block + lead)

        @pl.when((block < blocks) & gets_far)
        def _():
            far_copy(near, block).wait_recv()

        @pl.when(block >= 1)
        def _():
            march_block(block - 1)

    @pl.loop(0, blocks)
    def _(block):
        other_copy(block).wait_send()
        back_copy(block).wait_send()
        back_copy(block).wait_recv()

        @pl.when(has_after)
        def _():
            near_copy(block).wait_send()
            further_copy(block).wait_send()

        @pl.when(gives_far)
        def _():
            far_copy(near, block).wait_send()


def body(velocity, mean_flow, chol_diag, chol_off, eddy_x, eddy_y, eddy_z, eddy_signs, tile_lists):
    rows, columns = velocity.shape[2:]
    count = lax.axis_size("yz")
    slabs = lax.axis_size("gx")
    eddies = eddy_x.shape[0]
    blocks = rows // STRIDE
    cosine, low, sine = wall_bases(rows)
    table = mode_table(rows, columns, count)
    vmem = pl.BlockSpec(memory_space=pltpu.VMEM)
    hbm = pl.BlockSpec(memory_space=pl.ANY)
    half_plane = pltpu.VMEM((3, rows, columns // 2), jnp.bfloat16)
    square = pltpu.VMEM((rows, rows), jnp.bfloat16)
    lines = pltpu.VMEM((columns, rows), jnp.float32)
    lines16 = pltpu.VMEM((columns, rows), jnp.bfloat16)
    velocity_next, inflow = pl.pallas_call(
        functools.partial(step_kernel, slabs, count),
        out_shape=[
            jax.ShapeDtypeStruct((3, rows, columns), jnp.bfloat16),
            jax.ShapeDtypeStruct((3, rows, columns), jnp.float32),
        ],
        in_specs=[hbm] * 4 + [vmem] * 8,
        out_specs=[vmem, vmem],
        scratch_shapes=[half_plane] * 6
        + [square] * 3
        + [
            pltpu.VMEM((7, rows, LANES), jnp.float32),
            pltpu.VMEM((3, columns, eddies), jnp.bfloat16),
            pltpu.VMEM((3, 16, eddies), jnp.bfloat16),
            pltpu.VMEM((8, columns), jnp.float32),
            lines16, lines16, lines, lines, lines, lines16, lines16,
            pltpu.VMEM((count, 8, rows), jnp.float32),
            pltpu.SemaphoreType.DMA((4,)),
        ]
        + [pltpu.SemaphoreType.DMA((blocks,))] * 10
        + [pltpu.SemaphoreType.DMA((count - 1,))] * 2,
        compiler_params=pltpu.CompilerParams(
            collective_id=0, has_side_effects=True, vmem_limit_bytes=60 * 1024 * 1024
        ),
        cost_estimate=pl.CostEstimate(
            flops=2 * rows * columns * (3 * eddies + 5 * rows), bytes_accessed=24 * rows * columns, transcendentals=0
        ),
        name="step",
    )(
        velocity[:, 0], jnp.asarray(cosine), jnp.asarray(low), jnp.asarray(sine),
        mean_flow[None], chol_diag, chol_off, eddy_x[None], eddy_y[None], eddy_z[None], eddy_signs, jnp.asarray(table),
    )
    return velocity_next[:, None], inflow[None]


def solution(mesh):
    placed = (P(None, "gx", None, "yz"), P(), P(), P(), P(), P(), P(), P(), P("yz", None))
    return jax.shard_map(
        body,
        mesh=mesh,
        in_specs=placed,
        out_specs=(P(None, "gx", None, "yz"), P(None, None, None, "yz")),
        check_vma=False,
    )
```

```python
import functools
import math

import jax
import jax.numpy as jnp
import numpy as np
from jax import lax
from jax.experimental import pallas as pl
from jax.experimental.pallas import tpu as pltpu
from jax.sharding import PartitionSpec as P

TILE = 128
EPT = 96
SIGMA = 64
LANES = 128
STRIDE = 64
PIECE = 32
TILE_ROWS = 16
PAD = 32
BAND = 256
MESH = pl.DeviceIdType.MESH

shape_peak = math.sqrt(1.5)
time_step = 0.4
viscosity = 0.3

THETA, RATE, RATE2, RATE4, ALPHA, BETA, PERIOD, POWERS = range(8)


def tent_shape(ratio):
    return shape_peak * jnp.maximum(0.0, 1.0 - jnp.abs(ratio))


def wall_bases(rows):
    k = np.arange(rows)[None, :]
    y = np.arange(rows)[:, None]
    norm = np.where(k == 0, math.sqrt(1.0 / rows), math.sqrt(2.0 / rows))
    cosine = norm * np.cos((k * (2 * y + 1) % (4 * rows)) * (math.pi / (2 * rows)))
    sine = math.sqrt(2.0 / rows) * np.sin((k * (y + 1) % (2 * rows)) * (math.pi / rows))
    high = cosine.astype(jnp.bfloat16)
    low = (cosine - high.astype(np.float64)).astype(jnp.bfloat16)
    return high, low, sine.astype(jnp.bfloat16)


def mode_table(rows, length, count):
    theta = 2.0 * np.arcsinh(np.sin(np.arange(rows) * (math.pi / (2 * rows))))
    rate = np.exp(-theta)
    period = np.where(theta > 0, 1.0 / np.maximum(-np.expm1(-theta * length * count), 1e-30), 1.0)
    table = [theta, rate, rate**2, rate**4, rate / (1.0 + rate), np.sqrt(rate) / (1.0 + rate), period]
    table += [np.exp(-theta * length * q) for q in range(count)]
    table += [np.zeros(rows)] * (-len(table) % 8)
    return np.stack(table).astype(np.float32)


def dot(a, b, contract):
    return lax.dot_general(a, b, (contract, ((), ())), preferred_element_type=jnp.float32)


NN = ((1,), (0,))
NT = ((1,), (1,))


def step_kernel(
    slabs, count,
    vel_ref, cos_hbm, low_hbm, sin_hbm, mean_hbm, diag_hbm, off_hbm, x_hbm, y_hbm, z_hbm, sign_hbm, table_hbm,
    next_ref, flow_ref,
    mean_ref, diag_ref, off_ref, x_ref, y_ref, z_ref, sign_ref, table_ref,
    own, behind, far, back, state,
    cosine, cosine_low, sine, params, weight, edge_weight, carry_row,
    div_high, div_low, modes, ups, downs, slope_modes, rise_modes, sums,
    load_sem, other_send, other_recv, near_send, near_recv, further_send, further_recv,
    far_send, far_recv, back_send, back_recv, sum_send, sum_recv,
):
    rows, columns = flow_ref.shape[1:]
    half = columns // 2
    spanwise = columns * count
    eddies = sign_ref.shape[1]
    blocks = rows // STRIDE
    me = lax.axis_index("gx")
    pencil = lax.axis_index("yz")
    parity = lax.rem(me, 2)
    partner = me + 1 - 2 * parity
    has_after = me + 2 < slabs
    has_before = me >= 2
    gets_far = me >= 4
    gives_far = has_after & (me >= 2)
    after = jnp.where(has_after, me + 2, me - 2)
    at_inlet = me < 2
    after_inlet = (me >= 2) & (me < 4)
    mine_at = pl.multiple_of(parity * half, half)
    theirs_at = pl.multiple_of((1 - parity) * half, half)

    barrier = pltpu.get_barrier_semaphore()
    pl.semaphore_signal(barrier, inc=1, device_id={"gx": partner}, device_id_type=MESH)
    for step in range(1, count):
        pl.semaphore_signal(barrier, inc=1, device_id={"yz": lax.rem(pencil + step, count)}, device_id_type=MESH)

    @pl.when(has_after)
    def _():
        pl.semaphore_signal(barrier, inc=1, device_id={"gx": after}, device_id_type=MESH)

    @pl.when(has_before)
    def _():
        pl.semaphore_signal(barrier, inc=1, device_id={"gx": me - 2}, device_id_type=MESH)

    loads = [
        pltpu.make_async_copy(
            vel_ref.at[:, :, pl.ds(mine_at, half)], own.at[parity, :, pl.ds(0, rows), :], load_sem.at[0]
        ),
        pltpu.make_async_copy(cos_hbm, cosine, load_sem.at[1]),
        pltpu.make_async_copy(low_hbm, cosine_low, load_sem.at[2]),
        pltpu.make_async_copy(sin_hbm, sine, load_sem.at[3]),
    ]
    small = [
        pltpu.make_async_copy(source, target, load_sem.at[4 + at])
        for at, (source, target) in enumerate(
            [
                (mean_hbm, mean_ref), (diag_hbm, diag_ref), (off_hbm, off_ref), (x_hbm, x_ref),
                (y_hbm, y_ref), (z_hbm, z_ref), (sign_hbm, sign_ref), (table_hbm, table_ref),
            ]
        )
    ]
    for load in small + loads:
        load.start()

    pl.semaphore_wait(barrier, count + has_after.astype(jnp.int32) + has_before.astype(jnp.int32))

    def rows_of(block, size=STRIDE):
        return pl.ds(pl.multiple_of(block * size, size), size)

    def send(source, target, block, send_sem, recv_sem, device):
        return pltpu.make_async_remote_copy(
            src_ref=source,
            dst_ref=target,
            send_sem=send_sem.at[block],
            recv_sem=recv_sem.at[block],
            device_id={"gx": device},
            device_id_type=MESH,
        )

    def other_copy(block):
        here = rows_of(block)
        source = vel_ref.at[:, here, pl.ds(theirs_at, half)]
        return send(source, own.at[parity, :, here, :], block, other_send, other_recv, partner)

    def near_copy(block):
        here = rows_of(block)
        source = vel_ref.at[:, here, pl.ds(mine_at, half)]
        return send(source, behind.at[parity, :, here, :], block, near_send, near_recv, after)

    def further_copy(block):
        here = rows_of(block)
        source, target = own.at[1 - parity, :, here, :], behind.at[1 - parity, :, here, :]
        return send(source, target, block, further_send, further_recv, after)

    def far_copy(block):
        here = rows_of(block)
        return send(behind.at[1, :, here, :], far.at[:, here, :], block, far_send, far_recv, after)

    def back_copy(piece):
        here = rows_of(piece, PIECE)
        target = next_ref.at[:, here, pl.ds(mine_at, half)]
        return send(back.at[:, here, :], target, piece, back_send, back_recv, partner)

    @pl.loop(0, blocks)
    def _(block):
        other_copy(block).start()

        @pl.when(has_after)
        def _():
            near_copy(block).start()

    def start_further(block):
        other_copy(block).wait_recv()

        @pl.when(has_after)
        def _():
            further_copy(block).start()

    def start_far(block):
        @pl.when(has_before)
        def _():
            near_copy(block).wait_recv()
            further_copy(block).wait_recv()

        @pl.when(gives_far)
        def _():
            far_copy(block).start()

    beyond = pl.ds(rows, PAD)
    own[:, :, beyond, :] = jnp.zeros((2, 3, PAD, half), jnp.bfloat16)
    behind[:, :, beyond, :] = jnp.zeros((2, 3, PAD, half), jnp.bfloat16)
    far[:, beyond, :] = jnp.zeros((3, PAD, half), jnp.bfloat16)
    state[...] = jnp.zeros_like(state)

    @pl.when(at_inlet)
    def _():
        behind[0] = jnp.zeros_like(behind[0])
        far[...] = jnp.zeros_like(far)

    for load in small:
        load.wait()

    for edge in (0, PAD + rows):
        params[0, pl.ds(edge, PAD), :] = jnp.zeros((PAD, LANES), jnp.float32)
    for place, row in enumerate(
        [mean_ref[...].reshape(1, rows)] + [diag_ref[c : c + 1, :] for c in range(3)] + [off_ref[c : c + 1, :] for c in range(3)]
    ):
        params[place, pl.ds(PAD, rows), :] = jnp.transpose(jnp.broadcast_to(row, (LANES, rows)))

    first_cell = pencil * columns
    amplitude = math.sqrt(8.0 * rows / (TILE * EPT))
    eddy_x, eddy_y, eddy_z = (ref[...].reshape(1, eddies) for ref in (x_ref, y_ref, z_ref))
    stretch = amplitude * tent_shape(eddy_x.astype(jnp.float32) / SIGMA)
    scales = [stretch * (2 * sign_ref[j : j + 1, :] - 1).astype(jnp.float32) for j in range(3)]

    def weights(start, extent):
        cells = start + lax.broadcasted_iota(jnp.int32, (extent, eddies), 0)
        offset = cells - eddy_z
        offset = jnp.where(offset >= spanwise // 2, offset - spanwise, offset)
        offset = jnp.where(offset < -(spanwise // 2), offset + spanwise, offset)
        shape_z = tent_shape(offset.astype(jnp.float32) / SIGMA)
        return [(scale * shape_z).astype(jnp.bfloat16) for scale in scales]

    @pl.loop(0, columns // LANES)
    def _(tile):
        start = pl.multiple_of(tile * LANES, LANES)
        for j, value in enumerate(weights(first_cell + start, LANES)):
            weight[j, pl.ds(start, LANES), :] = value

    for j, value in enumerate(weights(jnp.where(pencil == 0, spanwise, first_cell) - 1, 16)):
        edge_weight[j] = value

    carry_row[...] = jnp.zeros_like(carry_row)

    @pl.loop(0, rows // BAND)
    def _(band):
        start = pl.multiple_of(band * BAND, BAND)
        here = pl.ds(start, BAND)
        cells = start + lax.broadcasted_iota(jnp.int32, (BAND, eddies), 0)
        shape_y = tent_shape((cells - eddy_y).astype(jnp.float32) / SIGMA).astype(jnp.bfloat16)
        fl = [dot(shape_y, weight[j], NT) for j in range(3)]
        ends = [dot(shape_y, edge_weight[j], NT)[:, 0:1] for j in range(3)]

        def spread(place):
            return jnp.concatenate([params[place, pl.ds(PAD + start, BAND), :]] * (columns // LANES), axis=1)

        flow_ref[0, here, :] = spread(0) + spread(1) * fl[0]
        row = start + lax.broadcasted_iota(jnp.int32, (BAND, columns), 0)
        flux = jnp.where(row == rows - 1, 0.0, spread(4) * fl[0] + spread(2) * fl[1])
        third = spread(5) * fl[0] + spread(6) * fl[1] + spread(3) * fl[2]
        edge = (
            params[5, pl.ds(PAD + start, BAND), 0:1] * ends[0] + params[6, pl.ds(PAD + start, BAND), 0:1] * ends[1] + params[3, pl.ds(PAD + start, BAND), 0:1] * ends[2]
        )
        lower = jnp.where(row == start, carry_row[0:1, :], pltpu.roll(flux, 1, 0))
        lane = lax.broadcasted_iota(jnp.int32, (BAND, columns), 1)
        previous = jnp.where(lane == 0, edge, pltpu.roll(third, 1, 1))
        carry_row[0:1, :] = flux[BAND - 1 : BAND, :]
        flow_ref[1, here, :] = flux
        flow_ref[2, here, :] = third
        div = jnp.transpose(flux - lower + third - previous)
        high = div.astype(jnp.bfloat16)
        div_high[:, here] = high
        div_low[:, here] = (div - high.astype(jnp.float32)).astype(jnp.bfloat16)

    loads[1].wait()
    loads[2].wait()

    @pl.loop(0, rows // BAND)
    def _(band):
        here = pl.ds(pl.multiple_of(band * BAND, BAND), BAND)
        wall = cosine[:, here]
        modes[:, here] = (
            dot(div_high[...], wall, NN) + dot(div_low[...], wall, NN) + dot(div_high[...], cosine_low[:, here], NN)
        )

    def entry(place):
        return table_ref[place : place + 1, :]

    line = lax.broadcasted_iota(jnp.int32, (8, rows), 0)
    line_f = line.astype(jnp.float32)
    theta, rate, rate2, rate4 = entry(THETA), entry(RATE), entry(RATE2), entry(RATE4)
    steps = columns // 8

    def scan_step(step, carry):
        up_carry, down_carry, run = carry
        at = pl.ds(pl.multiple_of(step * 8, 8), 8)
        value = modes[at, :]
        value = value + jnp.where(line >= 1, rate, 0.0) * pltpu.roll(value, 1, 0)
        value = value + jnp.where(line >= 2, rate2, 0.0) * pltpu.roll(value, 2, 0)
        value = value + jnp.where(line >= 4, rate4, 0.0) * pltpu.roll(value, 4, 0)
        value = value + jnp.exp(-theta * (line_f + 1.0)) * up_carry
        ups[at, :] = value
        at = pl.ds(pl.multiple_of((steps - 1 - step) * 8, 8), 8)
        down = modes[at, :]
        down = down + jnp.where(line < 7, rate, 0.0) * pltpu.roll(down, 7, 0)
        down = down + jnp.where(line < 6, rate2, 0.0) * pltpu.roll(down, 6, 0)
        down = down + jnp.where(line < 4, rate4, 0.0) * pltpu.roll(down, 4, 0)
        down = down + jnp.exp(-theta * (8.0 - line_f)) * down_carry
        downs[at, :] = jnp.where(line == 7, down_carry, pltpu.roll(down, 7, 0))
        return value[7:8, :], down[0:1, :], run + value

    zeros = jnp.zeros((1, rows), jnp.float32)
    sum_up, sum_down, run = lax.fori_loop(0, steps, scan_step, (zeros, zeros, jnp.zeros((8, rows), jnp.float32)))
    run = jnp.sum(run, axis=0, keepdims=True)
    sums[pencil] = jnp.where(line == 0, sum_up, jnp.where(line == 1, sum_down, run))

    def sum_copy(step):
        return pltpu.make_async_remote_copy(
            src_ref=sums.at[pencil],
            dst_ref=sums.at[pencil],
            send_sem=sum_send.at[step - 1],
            recv_sem=sum_recv.at[step - 1],
            device_id={"yz": lax.rem(pencil + step, count)},
            device_id_type=MESH,
        )

    for step in range(1, count):
        sum_copy(step).start()
    for step in range(1, count):
        sum_copy(step).wait_send()
        sum_copy(step).wait_recv()

    total_cells = float(spanwise)
    mean = sum(sums[p, 0:1, :] for p in range(count)) / total_cells
    carry_up, carry_down = zeros, zeros
    start, mine, before, shift = zeros, zeros, zeros, zeros
    for p in range(count):
        hops_up = lax.rem(pencil - 1 - p + 2 * count, count)
        hops_down = lax.rem(p - pencil - 1 + count, count)
        carry_up = carry_up + table_ref[pl.ds(POWERS + hops_up, 1), :] * sums[p, 0:1, :]
        carry_down = carry_down + table_ref[pl.ds(POWERS + hops_down, 1), :] * sums[p, 1:2, :]
        total = sums[p, 0:1, :] - mean * columns
        start = start + jnp.where(pencil == p, before, 0.0)
        mine = mine + jnp.where(pencil == p, total, 0.0)
        shift = shift + sums[p, 2:3, :] - mean * (columns * (columns + 1) / 2.0) + columns * before
        before = before + total
    start = start - shift / total_cells
    first = lax.broadcasted_iota(jnp.int32, (1, rows), 1) == 0
    carry_up = jnp.where(first, start, entry(PERIOD) * carry_up)
    carry_down = jnp.where(first, -start - mine, entry(PERIOD) * carry_down)
    mean = jnp.where(first, mean, 0.0)
    alpha, beta = entry(ALPHA), entry(BETA)

    @pl.loop(0, steps // 2)
    def _(step):
        slopes, rises = [], []
        for part in range(2):
            at = pl.ds(pl.multiple_of(step * 16 + part * 8, 8), 8)
            up_count = line_f + (step * 16 + part * 8 + 1).astype(jnp.float32)
            down_count = columns - up_count
            up = ups[at, :] + jnp.exp(-theta * up_count) * carry_up - mean * up_count
            down = downs[at, :] + jnp.exp(-theta * down_count) * carry_down - mean * down_count
            slopes.append(alpha * (up - down))
            rises.append(beta * (up + rate * down))
        at = pl.ds(pl.multiple_of(step * 16, 16), 16)
        slope_modes[at, :] = jnp.concatenate(slopes, axis=0).astype(jnp.bfloat16)
        rise_modes[at, :] = jnp.concatenate(rises, axis=0).astype(jnp.bfloat16)

    lead = min(4, blocks)
    for block in range(lead):
        start_further(block)

    loads[3].wait()

    @pl.loop(0, rows // BAND)
    def _(band):
        here = pl.ds(pl.multiple_of(band * BAND, BAND), BAND)
        flow_ref[2, here, :] = flow_ref[2, here, :] - dot(cosine[here, :], slope_modes[...], NT)
        flow_ref[1, here, :] = flow_ref[1, here, :] - dot(sine[here, :], rise_modes[...], NT)

    loads[0].wait()

    @pl.when(at_inlet)
    def _():
        behind[1, :, pl.ds(0, rows), :] = flow_ref[:, :, pl.ds(mine_at, half)].astype(jnp.bfloat16)

    @pl.when(after_inlet)
    def _():
        far[:, pl.ds(0, rows), :] = flow_ref[:, :, pl.ds(mine_at, half)].astype(jnp.bfloat16)

    sublane = lax.broadcasted_iota(jnp.int32, (8, LANES), 0)
    top, bottom = sublane == 0, sublane == 7
    lines_all = rows // 8

    def rate(mean, drag, before, centre, after, upstream):
        half_v = 0.5 * centre[1]
        up, down = viscosity - half_v, viscosity + half_v
        out = []
        for c in range(3):
            above = pltpu.roll(jnp.where(top, after[c], centre[c]), 7, 0)
            below = pltpu.roll(jnp.where(bottom, before[c], centre[c]), 1, 0)
            out.append(up * above + down * below + (mean * upstream[c] - drag * centre[c]))
        return out

    def plus(field, factor, change):
        return [u + factor * a for u, a in zip(field, change)]

    def rounded(field):
        return [a.astype(jnp.bfloat16).astype(jnp.float32) for a in field]

    def kept(flag, field):
        return [jnp.where(flag, a, 0.0) for a in field]

    def picked(first, second):
        return [jnp.where(at_inlet, a, b) for a, b in zip(first, second)]

    stage = (time_step * 8.0 / 15.0, time_step * 5.0 / 12.0, time_step * 0.75)
    undo = (-time_step * 17.0 / 60.0, -time_step * 5.0 / 12.0)

    def advance(line_at, carry, p0, p1, q0, q1, r1):
        means = [params[0, pl.ds(pl.multiple_of(PAD + (line_at - lag) * 8, 8), 8), :] for lag in (1, 2, 3)]
        drags = [mean + 2.0 * viscosity for mean in means]
        first_in = (line_at >= 1) & (line_at <= lines_all)
        second_in = (line_at >= 2) & (line_at <= lines_all + 1)
        (
            p0_b, p0_c, p1_b, p1_c, q0_b, q0_c, q1_b, q1_c, r1_c,
            q0_s1, q1_s1b, q1_s1c, q1_w1, q1_s2,
            p0_s1b, p0_s1c, p0_w1, p0_s2b, p0_s2c, p0_w2,
            p1_s1b, p1_s1c, p1_w1, p1_s2b, p1_s2c, p1_w2,
        ) = carry

        f = rate(means[0], drags[0], q0_b, q0_c, q0, r1_c)
        q0_s1a = rounded(plus(q0_c, stage[0], f))
        f = rate(means[0], drags[0], q1_b, q1_c, q1, q0_c)
        q1_s1a = kept(first_in, plus(q1_c, stage[0], f))
        q1_w1a = plus(q1_s1a, undo[0], f)
        f = rate(means[0], drags[0], p0_b, p0_c, p0, q1_c)
        p0_s1a = kept(first_in, plus(p0_c, stage[0], f))
        p0_w1a = plus(p0_s1a, undo[0], f)
        f = rate(means[0], drags[0], p1_b, p1_c, p1, p0_c)
        p1_s1a = kept(first_in, plus(p1_c, stage[0], f))
        p1_w1a = plus(p1_s1a, undo[0], f)

        f = rate(means[1], drags[1], q1_s1b, q1_s1c, q1_s1a, q0_s1)
        q1_s2a = rounded(plus(q1_w1, stage[1], f))
        f = rate(means[1], drags[1], p0_s1b, p0_s1c, p0_s1a, picked(q1_b, rounded(q1_s1c)))
        p0_s2a = kept(second_in, plus(p0_w1, stage[1], f))
        p0_w2a = plus(p0_s2a, undo[1], f)
        f = rate(means[1], drags[1], p1_s1b, p1_s1c, p1_s1a, rounded(p0_s1c))
        p1_s2a = kept(second_in, plus(p1_w1, stage[1], f))
        p1_w2a = plus(p1_s2a, undo[1], f)

        f = rate(means[2], drags[2], p0_s2b, p0_s2c, p0_s2a, q1_s2)
        p0_s3 = plus(p0_w2, stage[2], f)
        f = rate(means[2], drags[2], p1_s2b, p1_s2c, p1_s2a, rounded(p0_s2c))
        p1_s3 = plus(p1_w2, stage[2], f)

        carry = (
            p0_c, p0, p1_c, p1, q0_c, q0, q1_c, q1, r1,
            q0_s1a, q1_s1c, q1_s1a, q1_w1a, picked(q1_b, q1_s2a),
            p0_s1c, p0_s1a, p0_w1a, p0_s2c, p0_s2a, p0_w2a,
            p1_s1c, p1_s1a, p1_w1a, p1_s2c, p1_s2a, p1_w2a,
        )
        return carry, p0_s3, p1_s3

    fields = 26

    def march_block(block, tiles):
        @pl.loop(0, half // LANES)
        def _(column):
            lanes = pl.ds(pl.multiple_of(column * LANES, LANES), LANES)
            wide = pl.ds(pl.multiple_of(mine_at + column * LANES, LANES), LANES)

            def tile_step(i, held):
                tile = block * (STRIDE // TILE_ROWS) + i
                here = rows_of(tile, TILE_ROWS)
                there = rows_of(jnp.maximum(tile - 2, 0), TILE_ROWS)

                def load(ref):
                    values = [ref[c, here, lanes].astype(jnp.float32) for c in range(3)]
                    return [v[0:8] for v in values], [v[8:16] for v in values]

                inputs = [load(own.at[0]), load(own.at[1]), load(behind.at[0]), load(behind.at[1]), load(far)]
                carry, (p0_old, p1_old) = held
                carry, p0_low, p1_low = advance(2 * tile, carry, *[value[0] for value in inputs])
                carry, p0_new, p1_new = advance(2 * tile + 1, carry, *[value[1] for value in inputs])
                for c in range(3):
                    p0_out = jnp.concatenate([p0_old[c], p0_low[c]], axis=0).astype(jnp.bfloat16)
                    p1_out = jnp.concatenate([p1_old[c], p1_low[c]], axis=0).astype(jnp.bfloat16)
                    next_ref[c, there, wide] = jnp.where(parity == 0, p0_out, p1_out)
                    back[c, there, lanes] = jnp.where(parity == 0, p1_out, p0_out)
                return carry, (p0_new, p1_new)

            def restore(at):
                return [state[column, 3 * at + c] for c in range(3)]

            held = tuple(restore(at) for at in range(fields)), tuple(restore(fields + at) for at in range(2))
            carry, late = lax.fori_loop(0, tiles, tile_step, held)
            for at, field in enumerate(carry + late):
                for c in range(3):
                    state[column, 3 * at + c] = field[c]

    pieces = STRIDE // PIECE
    start_far(0)

    @pl.loop(0, blocks + 1)
    def _(block):
        @pl.when(block + 1 < blocks)
        def _():
            start_far(block + 1)

        @pl.when(block + lead < blocks)
        def _():
            start_further(block + lead)

        @pl.when((block < blocks) & gets_far)
        def _():
            far_copy(block).wait_recv()

        march_block(block, jnp.where(block < blocks, STRIDE // TILE_ROWS, PAD // TILE_ROWS))

        @pl.when(block >= 1)
        def _():
            back_copy(block * pieces - 1).start()

        @pl.when(block < blocks)
        def _():
            for piece in range(pieces - 1):
                back_copy(block * pieces + piece).start()

    @pl.loop(0, rows // PIECE)
    def _(piece):
        back_copy(piece).wait_send()
        back_copy(piece).wait_recv()

    @pl.loop(0, blocks)
    def _(block):
        other_copy(block).wait_send()

        @pl.when(has_after)
        def _():
            near_copy(block).wait_send()
            further_copy(block).wait_send()

        @pl.when(gives_far)
        def _():
            far_copy(block).wait_send()


def body(velocity, mean_flow, chol_diag, chol_off, eddy_x, eddy_y, eddy_z, eddy_signs, tile_lists):
    rows, columns = velocity.shape[2:]
    count = lax.axis_size("yz")
    slabs = lax.axis_size("gx")
    eddies = eddy_x.shape[0]
    blocks = rows // STRIDE
    cosine, low, sine = wall_bases(rows)
    table = mode_table(rows, columns, count)
    given = [
        velocity[:, 0], jnp.asarray(cosine), jnp.asarray(low), jnp.asarray(sine),
        mean_flow, chol_diag, chol_off, eddy_x, eddy_y, eddy_z, eddy_signs, jnp.asarray(table),
    ]
    small = [pltpu.VMEM(value.shape, value.dtype) for value in given[4:]]
    given = [pltpu.with_memory_space_constraint(value, pltpu.HBM) for value in given]
    vmem = pl.BlockSpec(memory_space=pltpu.VMEM)
    hbm = pl.BlockSpec(memory_space=pl.ANY)
    half = columns // 2
    pair = pltpu.VMEM((2, 3, rows + PAD, half), jnp.bfloat16)
    square = pltpu.VMEM((rows, rows), jnp.bfloat16)
    lines = pltpu.VMEM((columns, rows), jnp.float32)
    lines16 = pltpu.VMEM((columns, rows), jnp.bfloat16)
    velocity_next, inflow = pl.pallas_call(
        functools.partial(step_kernel, slabs, count),
        out_shape=[
            pltpu.VMEM((3, rows, columns), jnp.bfloat16),
            pltpu.VMEM((3, rows, columns), jnp.float32),
        ],
        in_specs=[hbm] * len(given),
        out_specs=[vmem, vmem],
        scratch_shapes=small
        + [
            pair,
            pair,
            pltpu.VMEM((3, rows + PAD, half), jnp.bfloat16),
            pltpu.VMEM((3, rows, half), jnp.bfloat16),
            pltpu.VMEM((half // LANES, 3 * 28, 8, LANES), jnp.float32),
        ]
        + [square] * 3
        + [
            pltpu.VMEM((7, rows + 2 * PAD, LANES), jnp.float32),
            pltpu.VMEM((3, columns, eddies), jnp.bfloat16),
            pltpu.VMEM((3, 16, eddies), jnp.bfloat16),
            pltpu.VMEM((8, columns), jnp.float32),
            lines16, lines16, lines, lines, lines, lines16, lines16,
            pltpu.VMEM((count, 8, rows), jnp.float32),
            pltpu.SemaphoreType.DMA((12,)),
        ]
        + [pltpu.SemaphoreType.DMA((blocks,))] * 8
        + [pltpu.SemaphoreType.DMA((rows // PIECE,))] * 2
        + [pltpu.SemaphoreType.DMA((count - 1,))] * 2,
        compiler_params=pltpu.CompilerParams(
            collective_id=0, has_side_effects=True, vmem_limit_bytes=48 * 1024 * 1024
        ),
        cost_estimate=pl.CostEstimate(
            flops=2 * rows * columns * (3 * eddies + 5 * rows), bytes_accessed=24 * rows * columns, transcendentals=0
        ),
        name="step",
    )(*given)
    return velocity_next[:, None], inflow[None]


def solution(mesh):
    placed = (P(None, "gx", None, "yz"), P(), P(), P(), P(), P(), P(), P(), P("yz", None))
    return jax.shard_map(
        body,
        mesh=mesh,
        in_specs=placed,
        out_specs=(P(None, "gx", None, "yz"), P(None, None, None, "yz")),
        check_vma=False,
    )
```

```python
import functools
import math

import jax
import jax.numpy as jnp
import numpy as np
from jax import lax
from jax.experimental import pallas as pl
from jax.experimental.pallas import tpu as pltpu
from jax.sharding import PartitionSpec as P

TILE = 128
EPT = 96
SIGMA = 64
LANES = 128
STRIDE = 64
PIECE = 32
TILE_ROWS = 16
PAD = 32
BAND = 256
MESH = pl.DeviceIdType.MESH

shape_peak = math.sqrt(1.5)
time_step = 0.4
viscosity = 0.3

THETA, RATE, RATE2, RATE4, ALPHA, BETA, PERIOD, POWERS = range(8)


def tent_shape(ratio):
    return shape_peak * jnp.maximum(0.0, 1.0 - jnp.abs(ratio))


def wall_bases(rows):
    k = np.arange(rows)[None, :]
    y = np.arange(rows)[:, None]
    norm = np.where(k == 0, math.sqrt(1.0 / rows), math.sqrt(2.0 / rows))
    cosine = norm * np.cos((k * (2 * y + 1) % (4 * rows)) * (math.pi / (2 * rows)))
    sine = math.sqrt(2.0 / rows) * np.sin((k * (y + 1) % (2 * rows)) * (math.pi / rows))
    high = cosine.astype(jnp.bfloat16)
    low = (cosine - high.astype(np.float64)).astype(jnp.bfloat16)
    return high, low, sine.astype(jnp.bfloat16)


def mode_table(rows, length, count):
    theta = 2.0 * np.arcsinh(np.sin(np.arange(rows) * (math.pi / (2 * rows))))
    rate = np.exp(-theta)
    period = np.where(theta > 0, 1.0 / np.maximum(-np.expm1(-theta * length * count), 1e-30), 1.0)
    table = [theta, rate, rate**2, rate**4, rate / (1.0 + rate), np.sqrt(rate) / (1.0 + rate), period]
    table += [np.exp(-theta * length * q) for q in range(count)]
    table += [np.zeros(rows)] * (-len(table) % 8)
    return np.stack(table).astype(np.float32)


def dot(a, b, contract):
    return lax.dot_general(a, b, (contract, ((), ())), preferred_element_type=jnp.float32)


NN = ((1,), (0,))
NT = ((1,), (1,))


def step_kernel(
    slabs, count,
    vel_ref, cos_hbm, low_hbm, sin_hbm, mean_hbm, diag_hbm, off_hbm, x_hbm, y_hbm, z_hbm, sign_hbm, table_hbm,
    next_ref, flow_ref,
    mean_ref, diag_ref, off_ref, x_ref, y_ref, z_ref, sign_ref, table_ref,
    own, behind, far, back, state,
    cosine, cosine_low, sine, params, weight, edge_weight, carry_row,
    div_high, div_low, modes, ups, downs, slope_modes, rise_modes, sums,
    load_sem, other_send, other_recv, near_send, near_recv, further_send, further_recv,
    far_send, far_recv, back_send, back_recv, sum_send, sum_recv,
):
    rows, columns = flow_ref.shape[1:]
    half = columns // 2
    spanwise = columns * count
    eddies = sign_ref.shape[1]
    blocks = rows // STRIDE
    me = lax.axis_index("gx")
    pencil = lax.axis_index("yz")
    parity = lax.rem(me, 2)
    partner = me + 1 - 2 * parity
    has_after = me + 2 < slabs
    has_before = me >= 2
    gets_far = me >= 4
    gives_far = has_after & (me >= 2)
    after = jnp.where(has_after, me + 2, me - 2)
    at_inlet = me < 2
    after_inlet = (me >= 2) & (me < 4)
    mine_at = pl.multiple_of(parity * half, half)
    theirs_at = pl.multiple_of((1 - parity) * half, half)

    barrier = pltpu.get_barrier_semaphore()
    pl.semaphore_signal(barrier, inc=1, device_id={"gx": partner}, device_id_type=MESH)
    for step in range(1, count):
        pl.semaphore_signal(barrier, inc=1, device_id={"yz": lax.rem(pencil + step, count)}, device_id_type=MESH)

    @pl.when(has_after)
    def _():
        pl.semaphore_signal(barrier, inc=1, device_id={"gx": after}, device_id_type=MESH)

    @pl.when(has_before)
    def _():
        pl.semaphore_signal(barrier, inc=1, device_id={"gx": me - 2}, device_id_type=MESH)

    loads = [
        pltpu.make_async_copy(
            vel_ref.at[:, :, pl.ds(mine_at, half)], own.at[parity, :, pl.ds(0, rows), :], load_sem.at[0]
        ),
        pltpu.make_async_copy(cos_hbm, cosine, load_sem.at[1]),
        pltpu.make_async_copy(low_hbm, cosine_low, load_sem.at[2]),
        pltpu.make_async_copy(sin_hbm, sine, load_sem.at[3]),
    ]
    small = [
        pltpu.make_async_copy(source, target, load_sem.at[4 + at])
        for at, (source, target) in enumerate(
            [
                (mean_hbm, mean_ref), (diag_hbm, diag_ref), (off_hbm, off_ref), (x_hbm, x_ref),
                (y_hbm, y_ref), (z_hbm, z_ref), (sign_hbm, sign_ref), (table_hbm, table_ref),
            ]
        )
    ]
    for load in small + loads:
        load.start()

    pl.semaphore_wait(barrier, count + has_after.astype(jnp.int32) + has_before.astype(jnp.int32))

    def rows_of(block, size=STRIDE):
        return pl.ds(pl.multiple_of(block * size, size), size)

    def send(source, target, send_sem, recv_sem, device):
        return pltpu.make_async_remote_copy(
            src_ref=source,
            dst_ref=target,
            send_sem=send_sem,
            recv_sem=recv_sem,
            device_id={"gx": device},
            device_id_type=MESH,
        )

    every = pl.ds(0, rows)

    def other_copy(block, here=None):
        here = rows_of(block) if here is None else here
        source = vel_ref.at[:, here, pl.ds(theirs_at, half)]
        return send(source, own.at[parity, :, here, :], other_send, other_recv.at[block], partner)

    def near_copy(block, here=None):
        here = rows_of(block) if here is None else here
        source = vel_ref.at[:, here, pl.ds(mine_at, half)]
        return send(source, behind.at[parity, :, here, :], near_send, near_recv.at[block], after)

    def further_copy(block, here=None):
        here = rows_of(block) if here is None else here
        source, target = own.at[1 - parity, :, here, :], behind.at[1 - parity, :, here, :]
        return send(source, target, further_send, further_recv.at[block], after)

    def far_copy(block, here=None):
        here = rows_of(block) if here is None else here
        return send(behind.at[1, :, here, :], far.at[:, here, :], far_send, far_recv.at[block], after)

    def back_copy(piece, here=None):
        here = rows_of(piece, PIECE) if here is None else here
        target = next_ref.at[:, here, pl.ds(mine_at, half)]
        return send(back.at[:, here, :], target, back_send, back_recv, partner)

    @pl.loop(0, blocks)
    def _(block):
        @pl.when(has_after)
        def _():
            near_copy(block).start()

        other_copy(block).start()

    def start_further(block):
        other_copy(block).wait_recv()

        @pl.when(has_after)
        def _():
            further_copy(block).start()

    def start_far(block):
        @pl.when(has_before)
        def _():
            near_copy(block).wait_recv()
            further_copy(block).wait_recv()

        @pl.when(gives_far)
        def _():
            far_copy(block).start()

    beyond = pl.ds(rows, PAD)
    own[:, :, beyond, :] = jnp.zeros((2, 3, PAD, half), jnp.bfloat16)
    behind[:, :, beyond, :] = jnp.zeros((2, 3, PAD, half), jnp.bfloat16)
    far[:, beyond, :] = jnp.zeros((3, PAD, half), jnp.bfloat16)
    state[...] = jnp.zeros_like(state)

    @pl.when(at_inlet)
    def _():
        behind[0] = jnp.zeros_like(behind[0])
        far[...] = jnp.zeros_like(far)

    for load in small:
        load.wait()

    for edge in (0, PAD + rows):
        params[0, pl.ds(edge, PAD), :] = jnp.zeros((PAD, LANES), jnp.float32)
    for place, row in enumerate(
        [mean_ref[...].reshape(1, rows)] + [diag_ref[c : c + 1, :] for c in range(3)] + [off_ref[c : c + 1, :] for c in range(3)]
    ):
        params[place, pl.ds(PAD, rows), :] = jnp.transpose(jnp.broadcast_to(row, (LANES, rows)))

    first_cell = pencil * columns
    amplitude = math.sqrt(8.0 * rows / (TILE * EPT))
    eddy_x, eddy_y, eddy_z = (ref[...].reshape(1, eddies) for ref in (x_ref, y_ref, z_ref))
    stretch = amplitude * tent_shape(eddy_x.astype(jnp.float32) / SIGMA)
    scales = [stretch * (2 * sign_ref[j : j + 1, :] - 1).astype(jnp.float32) for j in range(3)]

    def weights(start, extent):
        cells = start + lax.broadcasted_iota(jnp.int32, (extent, eddies), 0)
        offset = cells - eddy_z
        offset = jnp.where(offset >= spanwise // 2, offset - spanwise, offset)
        offset = jnp.where(offset < -(spanwise // 2), offset + spanwise, offset)
        shape_z = tent_shape(offset.astype(jnp.float32) / SIGMA)
        return [(scale * shape_z).astype(jnp.bfloat16) for scale in scales]

    @pl.loop(0, columns // LANES)
    def _(tile):
        start = pl.multiple_of(tile * LANES, LANES)
        for j, value in enumerate(weights(first_cell + start, LANES)):
            weight[j, pl.ds(start, LANES), :] = value

    for j, value in enumerate(weights(jnp.where(pencil == 0, spanwise, first_cell) - 1, 16)):
        edge_weight[j] = value

    carry_row[...] = jnp.zeros_like(carry_row)

    @pl.loop(0, rows // BAND)
    def _(band):
        start = pl.multiple_of(band * BAND, BAND)
        here = pl.ds(start, BAND)
        cells = start + lax.broadcasted_iota(jnp.int32, (BAND, eddies), 0)
        shape_y = tent_shape((cells - eddy_y).astype(jnp.float32) / SIGMA).astype(jnp.bfloat16)
        fl = [dot(shape_y, weight[j], NT) for j in range(3)]
        ends = [dot(shape_y, edge_weight[j], NT)[:, 0:1] for j in range(3)]

        def spread(place):
            return jnp.concatenate([params[place, pl.ds(PAD + start, BAND), :]] * (columns // LANES), axis=1)

        flow_ref[0, here, :] = spread(0) + spread(1) * fl[0]
        row = start + lax.broadcasted_iota(jnp.int32, (BAND, columns), 0)
        flux = jnp.where(row == rows - 1, 0.0, spread(4) * fl[0] + spread(2) * fl[1])
        third = spread(5) * fl[0] + spread(6) * fl[1] + spread(3) * fl[2]
        edge = (
            params[5, pl.ds(PAD + start, BAND), 0:1] * ends[0] + params[6, pl.ds(PAD + start, BAND), 0:1] * ends[1] + params[3, pl.ds(PAD + start, BAND), 0:1] * ends[2]
        )
        lower = jnp.where(row == start, carry_row[0:1, :], pltpu.roll(flux, 1, 0))
        lane = lax.broadcasted_iota(jnp.int32, (BAND, columns), 1)
        previous = jnp.where(lane == 0, edge, pltpu.roll(third, 1, 1))
        carry_row[0:1, :] = flux[BAND - 1 : BAND, :]
        flow_ref[1, here, :] = flux
        flow_ref[2, here, :] = third
        div = jnp.transpose(flux - lower + third - previous)
        high = div.astype(jnp.bfloat16)
        div_high[:, here] = high
        div_low[:, here] = (div - high.astype(jnp.float32)).astype(jnp.bfloat16)

    loads[1].wait()
    loads[2].wait()

    @pl.loop(0, rows // BAND)
    def _(band):
        here = pl.ds(pl.multiple_of(band * BAND, BAND), BAND)
        wall = cosine[:, here]
        modes[:, here] = (
            dot(div_high[...], wall, NN) + dot(div_low[...], wall, NN) + dot(div_high[...], cosine_low[:, here], NN)
        )

    def entry(place):
        return table_ref[place : place + 1, :]

    line = lax.broadcasted_iota(jnp.int32, (8, rows), 0)
    line_f = line.astype(jnp.float32)
    theta, rate, rate2, rate4 = entry(THETA), entry(RATE), entry(RATE2), entry(RATE4)
    steps = columns // 8

    def scan_step(step, carry):
        up_carry, down_carry, run = carry
        at = pl.ds(pl.multiple_of(step * 8, 8), 8)
        value = modes[at, :]
        value = value + jnp.where(line >= 1, rate, 0.0) * pltpu.roll(value, 1, 0)
        value = value + jnp.where(line >= 2, rate2, 0.0) * pltpu.roll(value, 2, 0)
        value = value + jnp.where(line >= 4, rate4, 0.0) * pltpu.roll(value, 4, 0)
        value = value + jnp.exp(-theta * (line_f + 1.0)) * up_carry
        ups[at, :] = value
        at = pl.ds(pl.multiple_of((steps - 1 - step) * 8, 8), 8)
        down = modes[at, :]
        down = down + jnp.where(line < 7, rate, 0.0) * pltpu.roll(down, 7, 0)
        down = down + jnp.where(line < 6, rate2, 0.0) * pltpu.roll(down, 6, 0)
        down = down + jnp.where(line < 4, rate4, 0.0) * pltpu.roll(down, 4, 0)
        down = down + jnp.exp(-theta * (8.0 - line_f)) * down_carry
        downs[at, :] = jnp.where(line == 7, down_carry, pltpu.roll(down, 7, 0))
        return value[7:8, :], down[0:1, :], run + value

    zeros = jnp.zeros((1, rows), jnp.float32)
    sum_up, sum_down, run = lax.fori_loop(0, steps, scan_step, (zeros, zeros, jnp.zeros((8, rows), jnp.float32)))
    run = jnp.sum(run, axis=0, keepdims=True)
    sums[pencil] = jnp.where(line == 0, sum_up, jnp.where(line == 1, sum_down, run))

    def sum_copy(step):
        return pltpu.make_async_remote_copy(
            src_ref=sums.at[pencil],
            dst_ref=sums.at[pencil],
            send_sem=sum_send.at[step - 1],
            recv_sem=sum_recv.at[step - 1],
            device_id={"yz": lax.rem(pencil + step, count)},
            device_id_type=MESH,
        )

    for step in range(1, count):
        sum_copy(step).start()
    for step in range(1, count):
        sum_copy(step).wait_send()
        sum_copy(step).wait_recv()

    total_cells = float(spanwise)
    mean = sum(sums[p, 0:1, :] for p in range(count)) / total_cells
    carry_up, carry_down = zeros, zeros
    start, mine, before, shift = zeros, zeros, zeros, zeros
    for p in range(count):
        hops_up = lax.rem(pencil - 1 - p + 2 * count, count)
        hops_down = lax.rem(p - pencil - 1 + count, count)
        carry_up = carry_up + table_ref[pl.ds(POWERS + hops_up, 1), :] * sums[p, 0:1, :]
        carry_down = carry_down + table_ref[pl.ds(POWERS + hops_down, 1), :] * sums[p, 1:2, :]
        total = sums[p, 0:1, :] - mean * columns
        start = start + jnp.where(pencil == p, before, 0.0)
        mine = mine + jnp.where(pencil == p, total, 0.0)
        shift = shift + sums[p, 2:3, :] - mean * (columns * (columns + 1) / 2.0) + columns * before
        before = before + total
    start = start - shift / total_cells
    first = lax.broadcasted_iota(jnp.int32, (1, rows), 1) == 0
    carry_up = jnp.where(first, start, entry(PERIOD) * carry_up)
    carry_down = jnp.where(first, -start - mine, entry(PERIOD) * carry_down)
    mean = jnp.where(first, mean, 0.0)
    alpha, beta = entry(ALPHA), entry(BETA)

    @pl.loop(0, steps // 2)
    def _(step):
        slopes, rises = [], []
        for part in range(2):
            at = pl.ds(pl.multiple_of(step * 16 + part * 8, 8), 8)
            up_count = line_f + (step * 16 + part * 8 + 1).astype(jnp.float32)
            down_count = columns - up_count
            up = ups[at, :] + jnp.exp(-theta * up_count) * carry_up - mean * up_count
            down = downs[at, :] + jnp.exp(-theta * down_count) * carry_down - mean * down_count
            slopes.append(alpha * (up - down))
            rises.append(beta * (up + rate * down))
        at = pl.ds(pl.multiple_of(step * 16, 16), 16)
        slope_modes[at, :] = jnp.concatenate(slopes, axis=0).astype(jnp.bfloat16)
        rise_modes[at, :] = jnp.concatenate(rises, axis=0).astype(jnp.bfloat16)

    @pl.loop(0, blocks)
    def _(block):
        start_further(block)

    loads[3].wait()

    @pl.loop(0, rows // BAND)
    def _(band):
        here = pl.ds(pl.multiple_of(band * BAND, BAND), BAND)
        flow_ref[2, here, :] = flow_ref[2, here, :] - dot(cosine[here, :], slope_modes[...], NT)
        flow_ref[1, here, :] = flow_ref[1, here, :] - dot(sine[here, :], rise_modes[...], NT)

    loads[0].wait()

    @pl.when(at_inlet)
    def _():
        behind[1, :, pl.ds(0, rows), :] = flow_ref[:, :, pl.ds(mine_at, half)].astype(jnp.bfloat16)

    @pl.when(after_inlet)
    def _():
        far[:, pl.ds(0, rows), :] = flow_ref[:, :, pl.ds(mine_at, half)].astype(jnp.bfloat16)

    sublane = lax.broadcasted_iota(jnp.int32, (8, LANES), 0)
    top, bottom = sublane == 0, sublane == 7
    lines_all = rows // 8

    def rate(mean, drag, before, centre, after, upstream):
        half_v = 0.5 * centre[1]
        up, down = viscosity - half_v, viscosity + half_v
        out = []
        for c in range(3):
            above = pltpu.roll(jnp.where(top, after[c], centre[c]), 7, 0)
            below = pltpu.roll(jnp.where(bottom, before[c], centre[c]), 1, 0)
            out.append(up * above + down * below + (mean * upstream[c] - drag * centre[c]))
        return out

    def plus(field, factor, change):
        return [u + factor * a for u, a in zip(field, change)]

    def rounded(field):
        return [a.astype(jnp.bfloat16).astype(jnp.float32) for a in field]

    def kept(flag, field):
        return [jnp.where(flag, a, 0.0) for a in field]

    def picked(first, second):
        return [jnp.where(at_inlet, a, b) for a, b in zip(first, second)]

    stage = (time_step * 8.0 / 15.0, time_step * 5.0 / 12.0, time_step * 0.75)
    undo = (-time_step * 17.0 / 60.0, -time_step * 5.0 / 12.0)

    def advance(line_at, carry, p0, p1, q0, q1, r1):
        means = [params[0, pl.ds(pl.multiple_of(PAD + (line_at - lag) * 8, 8), 8), :] for lag in (1, 2, 3)]
        drags = [mean + 2.0 * viscosity for mean in means]
        first_in = (line_at >= 1) & (line_at <= lines_all)
        second_in = (line_at >= 2) & (line_at <= lines_all + 1)
        (
            p0_b, p0_c, p1_b, p1_c, q0_b, q0_c, q1_b, q1_c, r1_c,
            q0_s1, q1_s1b, q1_s1c, q1_w1, q1_s2,
            p0_s1b, p0_s1c, p0_w1, p0_s2b, p0_s2c, p0_w2,
            p1_s1b, p1_s1c, p1_w1, p1_s2b, p1_s2c, p1_w2,
        ) = carry

        f = rate(means[0], drags[0], q0_b, q0_c, q0, r1_c)
        q0_s1a = rounded(plus(q0_c, stage[0], f))
        f = rate(means[0], drags[0], q1_b, q1_c, q1, q0_c)
        q1_s1a = kept(first_in, plus(q1_c, stage[0], f))
        q1_w1a = plus(q1_s1a, undo[0], f)
        f = rate(means[0], drags[0], p0_b, p0_c, p0, q1_c)
        p0_s1a = kept(first_in, plus(p0_c, stage[0], f))
        p0_w1a = plus(p0_s1a, undo[0], f)
        f = rate(means[0], drags[0], p1_b, p1_c, p1, p0_c)
        p1_s1a = kept(first_in, plus(p1_c, stage[0], f))
        p1_w1a = plus(p1_s1a, undo[0], f)

        f = rate(means[1], drags[1], q1_s1b, q1_s1c, q1_s1a, q0_s1)
        q1_s2a = rounded(plus(q1_w1, stage[1], f))
        f = rate(means[1], drags[1], p0_s1b, p0_s1c, p0_s1a, picked(q1_b, rounded(q1_s1c)))
        p0_s2a = kept(second_in, plus(p0_w1, stage[1], f))
        p0_w2a = plus(p0_s2a, undo[1], f)
        f = rate(means[1], drags[1], p1_s1b, p1_s1c, p1_s1a, rounded(p0_s1c))
        p1_s2a = kept(second_in, plus(p1_w1, stage[1], f))
        p1_w2a = plus(p1_s2a, undo[1], f)

        f = rate(means[2], drags[2], p0_s2b, p0_s2c, p0_s2a, q1_s2)
        p0_s3 = plus(p0_w2, stage[2], f)
        f = rate(means[2], drags[2], p1_s2b, p1_s2c, p1_s2a, rounded(p0_s2c))
        p1_s3 = plus(p1_w2, stage[2], f)

        carry = (
            p0_c, p0, p1_c, p1, q0_c, q0, q1_c, q1, r1,
            q0_s1a, q1_s1c, q1_s1a, q1_w1a, picked(q1_b, q1_s2a),
            p0_s1c, p0_s1a, p0_w1a, p0_s2c, p0_s2a, p0_w2a,
            p1_s1c, p1_s1a, p1_w1a, p1_s2c, p1_s2a, p1_w2a,
        )
        return carry, p0_s3, p1_s3

    fields = 26

    def march_block(block, tiles):
        @pl.loop(0, half // LANES)
        def _(column):
            lanes = pl.ds(pl.multiple_of(column * LANES, LANES), LANES)
            wide = pl.ds(pl.multiple_of(mine_at + column * LANES, LANES), LANES)

            def tile_step(i, held):
                tile = block * (STRIDE // TILE_ROWS) + i
                here = rows_of(tile, TILE_ROWS)
                there = rows_of(jnp.maximum(tile - 2, 0), TILE_ROWS)

                def load(ref):
                    values = [ref[c, here, lanes].astype(jnp.float32) for c in range(3)]
                    return [v[0:8] for v in values], [v[8:16] for v in values]

                inputs = [load(own.at[0]), load(own.at[1]), load(behind.at[0]), load(behind.at[1]), load(far)]
                carry, (p0_old, p1_old) = held
                carry, p0_low, p1_low = advance(2 * tile, carry, *[value[0] for value in inputs])
                carry, p0_new, p1_new = advance(2 * tile + 1, carry, *[value[1] for value in inputs])
                for c in range(3):
                    p0_out = jnp.concatenate([p0_old[c], p0_low[c]], axis=0).astype(jnp.bfloat16)
                    p1_out = jnp.concatenate([p1_old[c], p1_low[c]], axis=0).astype(jnp.bfloat16)
                    next_ref[c, there, wide] = jnp.where(parity == 0, p0_out, p1_out)
                    back[c, there, lanes] = jnp.where(parity == 0, p1_out, p0_out)
                return carry, (p0_new, p1_new)

            def restore(at):
                return [state[column, 3 * at + c] for c in range(3)]

            held = tuple(restore(at) for at in range(fields)), tuple(restore(fields + at) for at in range(2))
            carry, late = lax.fori_loop(0, tiles, tile_step, held)
            for at, field in enumerate(carry + late):
                for c in range(3):
                    state[column, 3 * at + c] = field[c]

    pieces = STRIDE // PIECE
    lead = min(6, blocks)

    @pl.loop(0, lead)
    def _(block):
        start_far(block)

    @pl.loop(0, blocks + 1)
    def _(block):
        @pl.when(block + lead < blocks)
        def _():
            start_far(block + lead)

        @pl.when((block < blocks) & gets_far)
        def _():
            far_copy(block).wait_recv()

        march_block(block, jnp.where(block < blocks, STRIDE // TILE_ROWS, PAD // TILE_ROWS))

        @pl.when(block >= 1)
        def _():
            back_copy(block * pieces - 1).start()

        @pl.when(block < blocks)
        def _():
            for piece in range(pieces - 1):
                back_copy(block * pieces + piece).start()

    other_copy(0, every).wait_send()

    @pl.when(has_after)
    def _():
        near_copy(0, every).wait_send()
        further_copy(0, every).wait_send()

    @pl.when(gives_far)
    def _():
        far_copy(0, every).wait_send()

    back_copy(0, every).wait_send()
    back_copy(0, every).wait_recv()


def leave_kernel(next_ref, flow_ref, next_out, flow_out, sem):
    copies = []
    for c in range(3):
        copies.append(pltpu.make_async_copy(flow_ref.at[c], flow_out.at[c], sem.at[c]))
        copies.append(pltpu.make_async_copy(next_ref.at[c], next_out.at[c], sem.at[3 + c]))
    for copy in copies:
        copy.start()
    for copy in copies:
        copy.wait()


def body(velocity, mean_flow, chol_diag, chol_off, eddy_x, eddy_y, eddy_z, eddy_signs, tile_lists):
    rows, columns = velocity.shape[2:]
    count = lax.axis_size("yz")
    slabs = lax.axis_size("gx")
    eddies = eddy_x.shape[0]
    blocks = rows // STRIDE
    cosine, low, sine = wall_bases(rows)
    table = mode_table(rows, columns, count)
    given = [
        velocity[:, 0], jnp.asarray(cosine), jnp.asarray(low), jnp.asarray(sine),
        mean_flow, chol_diag, chol_off, eddy_x, eddy_y, eddy_z, eddy_signs, jnp.asarray(table),
    ]
    small = [pltpu.VMEM(value.shape, value.dtype) for value in given[4:]]
    given = [pltpu.with_memory_space_constraint(value, pltpu.HBM) for value in given]
    vmem = pl.BlockSpec(memory_space=pltpu.VMEM)
    hbm = pl.BlockSpec(memory_space=pl.ANY)
    half = columns // 2
    pair = pltpu.VMEM((2, 3, rows + PAD, half), jnp.bfloat16)
    square = pltpu.VMEM((rows, rows), jnp.bfloat16)
    lines = pltpu.VMEM((columns, rows), jnp.float32)
    lines16 = pltpu.VMEM((columns, rows), jnp.bfloat16)
    velocity_next, inflow = pl.pallas_call(
        functools.partial(step_kernel, slabs, count),
        out_shape=[
            pltpu.VMEM((3, rows, columns), jnp.bfloat16),
            pltpu.VMEM((3, rows, columns), jnp.float32),
        ],
        in_specs=[hbm] * len(given),
        out_specs=[vmem, vmem],
        scratch_shapes=small
        + [
            pair,
            pair,
            pltpu.VMEM((3, rows + PAD, half), jnp.bfloat16),
            pltpu.VMEM((3, rows, half), jnp.bfloat16),
            pltpu.VMEM((half // LANES, 3 * 28, 8, LANES), jnp.float32),
        ]
        + [square] * 3
        + [
            pltpu.VMEM((7, rows + 2 * PAD, LANES), jnp.float32),
            pltpu.VMEM((3, columns, eddies), jnp.bfloat16),
            pltpu.VMEM((3, 16, eddies), jnp.bfloat16),
            pltpu.VMEM((8, columns), jnp.float32),
            lines16, lines16, lines, lines, lines, lines16, lines16,
            pltpu.VMEM((count, 8, rows), jnp.float32),
            pltpu.SemaphoreType.DMA((12,)),
        ]
        + [pltpu.SemaphoreType.DMA(()), pltpu.SemaphoreType.DMA((blocks,))] * 4
        + [pltpu.SemaphoreType.DMA(())] * 2
        + [pltpu.SemaphoreType.DMA((count - 1,))] * 2,
        compiler_params=pltpu.CompilerParams(
            collective_id=0, has_side_effects=True, vmem_limit_bytes=48 * 1024 * 1024
        ),
        cost_estimate=pl.CostEstimate(
            flops=2 * rows * columns * (3 * eddies + 5 * rows), bytes_accessed=24 * rows * columns, transcendentals=0
        ),
        name="step",
    )(*given)
    velocity_next, inflow = pl.pallas_call(
        leave_kernel,
        out_shape=[
            jax.ShapeDtypeStruct(velocity_next.shape, jnp.bfloat16),
            jax.ShapeDtypeStruct(inflow.shape, jnp.float32),
        ],
        in_specs=[vmem, vmem],
        out_specs=[hbm, hbm],
        scratch_shapes=[pltpu.SemaphoreType.DMA((6,))],
        compiler_params=pltpu.CompilerParams(vmem_limit_bytes=1024 * 1024),
        cost_estimate=pl.CostEstimate(flops=0, bytes_accessed=36 * rows * columns, transcendentals=0),
        name="leave",
    )(*(pltpu.with_memory_space_constraint(value, pltpu.VMEM) for value in (velocity_next, inflow)))
    return velocity_next[:, None], inflow[None]


def solution(mesh):
    placed = (P(None, "gx", None, "yz"), P(), P(), P(), P(), P(), P(), P(), P("yz", None))
    return jax.shard_map(
        body,
        mesh=mesh,
        in_specs=placed,
        out_specs=(P(None, "gx", None, "yz"), P(None, None, None, "yz")),
        check_vma=False,
    )
```

```python
import functools
import math

import jax
import jax.numpy as jnp
import numpy as np
from jax import lax
from jax.experimental import pallas as pl
from jax.experimental.pallas import tpu as pltpu
from jax.sharding import PartitionSpec as P

TILE = 128
EPT = 96
SIGMA = 64
LANES = 128
STRIDE = 64
PIECE = 32
FINE = 32
TILE_ROWS = 16
PAD = 32
BAND = 256
MESH = pl.DeviceIdType.MESH

shape_peak = math.sqrt(1.5)
time_step = 0.4
viscosity = 0.3

THETA, RATE, RATE2, RATE4, ALPHA, BETA, PERIOD, POWERS = range(8)


def tent_shape(ratio):
    return shape_peak * jnp.maximum(0.0, 1.0 - jnp.abs(ratio))


def wall_bases(rows):
    k = np.arange(rows)[None, :]
    y = np.arange(rows)[:, None]
    norm = np.where(k == 0, math.sqrt(1.0 / rows), math.sqrt(2.0 / rows))
    cosine = norm * np.cos((k * (2 * y + 1) % (4 * rows)) * (math.pi / (2 * rows)))
    sine = math.sqrt(2.0 / rows) * np.sin((k * (y + 1) % (2 * rows)) * (math.pi / rows))
    high = cosine.astype(jnp.bfloat16)
    low = (cosine - high.astype(np.float64)).astype(jnp.bfloat16)
    return high, low, sine.astype(jnp.bfloat16)


def mode_table(rows, length, count):
    theta = 2.0 * np.arcsinh(np.sin(np.arange(rows) * (math.pi / (2 * rows))))
    rate = np.exp(-theta)
    period = np.where(theta > 0, 1.0 / np.maximum(-np.expm1(-theta * length * count), 1e-30), 1.0)
    table = [theta, rate, rate**2, rate**4, rate / (1.0 + rate), np.sqrt(rate) / (1.0 + rate), period]
    table += [np.exp(-theta * length * q) for q in range(count)]
    table += [np.zeros(rows)] * (-len(table) % 8)
    return np.stack(table).astype(np.float32)


def dot(a, b, contract):
    return lax.dot_general(a, b, (contract, ((), ())), preferred_element_type=jnp.float32)


NN = ((1,), (0,))
NT = ((1,), (1,))


def step_kernel(
    slabs, count,
    vel_ref, cos_hbm, low_hbm, sin_hbm, mean_hbm, diag_hbm, off_hbm, x_hbm, y_hbm, z_hbm, sign_hbm, table_hbm,
    next_ref, flow_ref,
    mean_ref, diag_ref, off_ref, x_ref, y_ref, z_ref, sign_ref, table_ref,
    own, behind, far, done, state, base,
    cosine, cosine_low, sine, params, weight, edge_weight, carry_row,
    div_high, div_low, modes, ups, downs, slope_modes, rise_modes, sums,
    load_sem, other_send, other_recv, near_send, near_recv, further_send, further_recv,
    far_send, far_recv, across_send, back_send, back_recv, own_sem, sum_send, sum_recv,
):
    rows, columns = flow_ref.shape[1:]
    half = columns // 2
    spanwise = columns * count
    eddies = sign_ref.shape[1]
    blocks = rows // STRIDE
    me = lax.axis_index("gx")
    pencil = lax.axis_index("yz")
    parity = lax.rem(me, 2)
    partner = me + 1 - 2 * parity
    has_after = me + 2 < slabs
    has_before = me >= 2
    gets_far = me >= 4
    gives_far = has_after & (me >= 2)
    gives_across = has_after & (parity == 0)
    across = jnp.where(has_after, me + 3, me - 1)
    after = jnp.where(has_after, me + 2, me - 2)
    at_inlet = me < 2
    after_inlet = (me >= 2) & (me < 4)
    mine_at = pl.multiple_of(parity * half, half)
    theirs_at = pl.multiple_of((1 - parity) * half, half)

    barrier = pltpu.get_barrier_semaphore()
    pl.semaphore_signal(barrier, inc=1, device_id={"gx": partner}, device_id_type=MESH)
    for step in range(1, count):
        pl.semaphore_signal(barrier, inc=1, device_id={"yz": lax.rem(pencil + step, count)}, device_id_type=MESH)

    @pl.when(has_after)
    def _():
        pl.semaphore_signal(barrier, inc=1, device_id={"gx": after}, device_id_type=MESH)

    @pl.when(has_before)
    def _():
        pl.semaphore_signal(barrier, inc=1, device_id={"gx": me - 2}, device_id_type=MESH)

    @pl.when(has_before & (parity == 1))
    def _():
        pl.semaphore_signal(barrier, inc=1, device_id={"gx": me - 3}, device_id_type=MESH)

    loads = [
        pltpu.make_async_copy(
            vel_ref.at[:, :, pl.ds(mine_at, half)], own.at[parity, :, pl.ds(0, rows), :], load_sem.at[0]
        ),
        pltpu.make_async_copy(cos_hbm, cosine, load_sem.at[1]),
        pltpu.make_async_copy(low_hbm, cosine_low, load_sem.at[2]),
        pltpu.make_async_copy(sin_hbm, sine, load_sem.at[3]),
    ]
    small = [
        pltpu.make_async_copy(source, target, load_sem.at[4 + at])
        for at, (source, target) in enumerate(
            [
                (mean_hbm, mean_ref), (diag_hbm, diag_ref), (off_hbm, off_ref), (x_hbm, x_ref),
                (y_hbm, y_ref), (z_hbm, z_ref), (sign_hbm, sign_ref), (table_hbm, table_ref),
            ]
        )
    ]
    for load in small + loads:
        load.start()

    pl.semaphore_wait(
        barrier,
        count + has_after.astype(jnp.int32) + has_before.astype(jnp.int32) + gives_across.astype(jnp.int32),
    )

    def rows_of(block, size=STRIDE):
        return pl.ds(pl.multiple_of(block * size, size), size)

    def send(source, target, send_sem, recv_sem, device):
        return pltpu.make_async_remote_copy(
            src_ref=source,
            dst_ref=target,
            send_sem=send_sem,
            recv_sem=recv_sem,
            device_id={"gx": device},
            device_id_type=MESH,
        )

    every = pl.ds(0, rows)

    def other_copy(block, here=None):
        here = rows_of(block) if here is None else here
        source = vel_ref.at[:, here, pl.ds(theirs_at, half)]
        return send(source, own.at[parity, :, here, :], other_send, other_recv.at[block], partner)

    def near_copy(block, here=None):
        here = rows_of(block) if here is None else here
        source = vel_ref.at[:, here, pl.ds(mine_at, half)]
        return send(source, behind.at[parity, :, here, :], near_send, near_recv.at[block], after)

    def further_copy(block, here=None):
        here = rows_of(block) if here is None else here
        source, target = own.at[1 - parity, :, here, :], behind.at[1 - parity, :, here, :]
        return send(source, target, further_send, further_recv.at[block], after)

    def across_copy(block):
        here = rows_of(block)
        source, target = vel_ref.at[:, here, pl.ds(theirs_at, half)], behind.at[parity, :, here, :]
        return send(source, target, across_send, further_recv.at[block], across)

    def far_copy(block, here=None):
        here = rows_of(block, FINE) if here is None else here
        return send(behind.at[1, :, here, :], far.at[:, here, :], far_send, far_recv.at[block], after)

    def back_copy(here):
        target = next_ref.at[:, here, pl.ds(mine_at, half)]
        return send(done.at[1 - parity, :, here, :], target, back_send, back_recv, partner)

    def own_copy(plane, here):
        return pltpu.make_async_copy(
            done.at[plane, :, here, :], next_ref.at[:, here, pl.ds(mine_at, half)], own_sem
        )

    def leave(plane, here):
        @pl.when(parity == plane)
        def _():
            own_copy(plane, here).start()

        @pl.when(parity != plane)
        def _():
            back_copy(here).start()

    @pl.loop(0, blocks)
    def _(block):
        @pl.when(has_after)
        def _():
            near_copy(block).start()

        other_copy(block).start()

    crossing = 1

    @pl.when(gives_across)
    def _():
        for block in range(crossing):
            across_copy(block).start()

    def start_further(block):
        other_copy(block).wait_recv()

        @pl.when(has_after & ((parity == 0) | (block >= crossing)))
        def _():
            further_copy(block).start()

    def start_far(block):
        @pl.when(has_before)
        def _():
            near_copy(block).wait_recv()
            further_copy(block).wait_recv()

        @pl.when(gives_far)
        def _():
            for part in range(STRIDE // FINE):
                far_copy(block * (STRIDE // FINE) + part).start()

    beyond = pl.ds(rows, PAD)
    own[:, :, beyond, :] = jnp.zeros((2, 3, PAD, half), jnp.bfloat16)
    behind[:, :, beyond, :] = jnp.zeros((2, 3, PAD, half), jnp.bfloat16)
    far[:, beyond, :] = jnp.zeros((3, PAD, half), jnp.bfloat16)
    state[...] = jnp.zeros_like(state)

    @pl.when(at_inlet)
    def _():
        behind[0] = jnp.zeros_like(behind[0])
        far[...] = jnp.zeros_like(far)

    for load in small:
        load.wait()

    for edge in (0, PAD + rows):
        params[0, pl.ds(edge, PAD), :] = jnp.zeros((PAD, LANES), jnp.float32)
    for place, row in enumerate(
        [mean_ref[...].reshape(1, rows)] + [diag_ref[c : c + 1, :] for c in range(3)] + [off_ref[c : c + 1, :] for c in range(3)]
    ):
        params[place, pl.ds(PAD, rows), :] = jnp.transpose(jnp.broadcast_to(row, (LANES, rows)))

    first_cell = pencil * columns
    amplitude = math.sqrt(8.0 * rows / (TILE * EPT))
    eddy_x, eddy_y, eddy_z = (ref[...].reshape(1, eddies) for ref in (x_ref, y_ref, z_ref))
    stretch = amplitude * tent_shape(eddy_x.astype(jnp.float32) / SIGMA)
    scales = [stretch * (2 * sign_ref[j : j + 1, :] - 1).astype(jnp.float32) for j in range(3)]

    def weights(start, extent):
        cells = start + lax.broadcasted_iota(jnp.int32, (extent, eddies), 0)
        offset = cells - eddy_z
        offset = jnp.where(offset >= spanwise // 2, offset - spanwise, offset)
        offset = jnp.where(offset < -(spanwise // 2), offset + spanwise, offset)
        shape_z = tent_shape(offset.astype(jnp.float32) / SIGMA)
        return [(scale * shape_z).astype(jnp.bfloat16) for scale in scales]

    @pl.loop(0, columns // LANES)
    def _(tile):
        start = pl.multiple_of(tile * LANES, LANES)
        for j, value in enumerate(weights(first_cell + start, LANES)):
            weight[j, pl.ds(start, LANES), :] = value

    for j, value in enumerate(weights(jnp.where(pencil == 0, spanwise, first_cell) - 1, 16)):
        edge_weight[j] = value

    carry_row[...] = jnp.zeros_like(carry_row)

    @pl.loop(0, rows // BAND)
    def _(band):
        start = pl.multiple_of(band * BAND, BAND)
        here = pl.ds(start, BAND)
        cells = start + lax.broadcasted_iota(jnp.int32, (BAND, eddies), 0)
        shape_y = tent_shape((cells - eddy_y).astype(jnp.float32) / SIGMA).astype(jnp.bfloat16)
        fl = [dot(shape_y, weight[j], NT) for j in range(3)]
        ends = [dot(shape_y, edge_weight[j], NT)[:, 0:1] for j in range(3)]

        def spread(place):
            return jnp.concatenate([params[place, pl.ds(PAD + start, BAND), :]] * (columns // LANES), axis=1)

        flow_ref[0, here, :] = spread(0) + spread(1) * fl[0]
        row = start + lax.broadcasted_iota(jnp.int32, (BAND, columns), 0)
        flux = jnp.where(row == rows - 1, 0.0, spread(4) * fl[0] + spread(2) * fl[1])
        third = spread(5) * fl[0] + spread(6) * fl[1] + spread(3) * fl[2]
        edge = (
            params[5, pl.ds(PAD + start, BAND), 0:1] * ends[0] + params[6, pl.ds(PAD + start, BAND), 0:1] * ends[1] + params[3, pl.ds(PAD + start, BAND), 0:1] * ends[2]
        )
        lower = jnp.where(row == start, carry_row[0:1, :], pltpu.roll(flux, 1, 0))
        lane = lax.broadcasted_iota(jnp.int32, (BAND, columns), 1)
        previous = jnp.where(lane == 0, edge, pltpu.roll(third, 1, 1))
        carry_row[0:1, :] = flux[BAND - 1 : BAND, :]
        flow_ref[1, here, :] = flux
        flow_ref[2, here, :] = third
        div = jnp.transpose(flux - lower + third - previous)
        high = div.astype(jnp.bfloat16)
        div_high[:, here] = high
        div_low[:, here] = (div - high.astype(jnp.float32)).astype(jnp.bfloat16)

    loads[1].wait()
    loads[2].wait()

    @pl.loop(0, rows // BAND)
    def _(band):
        here = pl.ds(pl.multiple_of(band * BAND, BAND), BAND)
        wall = cosine[:, here]
        modes[:, here] = (
            dot(div_high[...], wall, NN) + dot(div_low[...], wall, NN) + dot(div_high[...], cosine_low[:, here], NN)
        )

    def entry(place):
        return table_ref[place : place + 1, :]

    line = lax.broadcasted_iota(jnp.int32, (8, rows), 0)
    line_f = line.astype(jnp.float32)
    theta, rate, rate2, rate4 = entry(THETA), entry(RATE), entry(RATE2), entry(RATE4)
    steps = columns // 8

    def scan_step(step, carry):
        up_carry, down_carry, run = carry
        at = pl.ds(pl.multiple_of(step * 8, 8), 8)
        value = modes[at, :]
        value = value + jnp.where(line >= 1, rate, 0.0) * pltpu.roll(value, 1, 0)
        value = value + jnp.where(line >= 2, rate2, 0.0) * pltpu.roll(value, 2, 0)
        value = value + jnp.where(line >= 4, rate4, 0.0) * pltpu.roll(value, 4, 0)
        value = value + jnp.exp(-theta * (line_f + 1.0)) * up_carry
        ups[at, :] = value
        at = pl.ds(pl.multiple_of((steps - 1 - step) * 8, 8), 8)
        down = modes[at, :]
        down = down + jnp.where(line < 7, rate, 0.0) * pltpu.roll(down, 7, 0)
        down = down + jnp.where(line < 6, rate2, 0.0) * pltpu.roll(down, 6, 0)
        down = down + jnp.where(line < 4, rate4, 0.0) * pltpu.roll(down, 4, 0)
        down = down + jnp.exp(-theta * (8.0 - line_f)) * down_carry
        downs[at, :] = jnp.where(line == 7, down_carry, pltpu.roll(down, 7, 0))
        return value[7:8, :], down[0:1, :], run + value

    zeros = jnp.zeros((1, rows), jnp.float32)
    sum_up, sum_down, run = lax.fori_loop(0, steps, scan_step, (zeros, zeros, jnp.zeros((8, rows), jnp.float32)))
    run = jnp.sum(run, axis=0, keepdims=True)
    sums[pencil] = jnp.where(line == 0, sum_up, jnp.where(line == 1, sum_down, run))

    def sum_copy(step):
        return pltpu.make_async_remote_copy(
            src_ref=sums.at[pencil],
            dst_ref=sums.at[pencil],
            send_sem=sum_send.at[step - 1],
            recv_sem=sum_recv.at[step - 1],
            device_id={"yz": lax.rem(pencil + step, count)},
            device_id_type=MESH,
        )

    for step in range(1, count):
        sum_copy(step).start()
    for step in range(1, count):
        sum_copy(step).wait_send()
        sum_copy(step).wait_recv()

    total_cells = float(spanwise)
    mean = sum(sums[p, 0:1, :] for p in range(count)) / total_cells
    carry_up, carry_down = zeros, zeros
    start, mine, before, shift = zeros, zeros, zeros, zeros
    for p in range(count):
        hops_up = lax.rem(pencil - 1 - p + 2 * count, count)
        hops_down = lax.rem(p - pencil - 1 + count, count)
        carry_up = carry_up + table_ref[pl.ds(POWERS + hops_up, 1), :] * sums[p, 0:1, :]
        carry_down = carry_down + table_ref[pl.ds(POWERS + hops_down, 1), :] * sums[p, 1:2, :]
        total = sums[p, 0:1, :] - mean * columns
        start = start + jnp.where(pencil == p, before, 0.0)
        mine = mine + jnp.where(pencil == p, total, 0.0)
        shift = shift + sums[p, 2:3, :] - mean * (columns * (columns + 1) / 2.0) + columns * before
        before = before + total
    start = start - shift / total_cells
    first = lax.broadcasted_iota(jnp.int32, (1, rows), 1) == 0
    carry_up = jnp.where(first, start, entry(PERIOD) * carry_up)
    carry_down = jnp.where(first, -start - mine, entry(PERIOD) * carry_down)
    mean = jnp.where(first, mean, 0.0)
    alpha, beta = entry(ALPHA), entry(BETA)

    @pl.loop(0, steps // 2)
    def _(step):
        slopes, rises = [], []
        for part in range(2):
            at = pl.ds(pl.multiple_of(step * 16 + part * 8, 8), 8)
            up_count = line_f + (step * 16 + part * 8 + 1).astype(jnp.float32)
            down_count = columns - up_count
            up = ups[at, :] + jnp.exp(-theta * up_count) * carry_up - mean * up_count
            down = downs[at, :] + jnp.exp(-theta * down_count) * carry_down - mean * down_count
            slopes.append(alpha * (up - down))
            rises.append(beta * (up + rate * down))
        at = pl.ds(pl.multiple_of(step * 16, 16), 16)
        slope_modes[at, :] = jnp.concatenate(slopes, axis=0).astype(jnp.bfloat16)
        rise_modes[at, :] = jnp.concatenate(rises, axis=0).astype(jnp.bfloat16)

    @pl.loop(0, blocks)
    def _(block):
        start_further(block)

    loads[3].wait()

    @pl.loop(0, rows // BAND)
    def _(band):
        here = pl.ds(pl.multiple_of(band * BAND, BAND), BAND)
        flow_ref[2, here, :] = flow_ref[2, here, :] - dot(cosine[here, :], slope_modes[...], NT)
        flow_ref[1, here, :] = flow_ref[1, here, :] - dot(sine[here, :], rise_modes[...], NT)

    loads[0].wait()

    @pl.when(at_inlet)
    def _():
        behind[1, :, pl.ds(0, rows), :] = flow_ref[:, :, pl.ds(mine_at, half)].astype(jnp.bfloat16)

    @pl.when(after_inlet)
    def _():
        far[:, pl.ds(0, rows), :] = flow_ref[:, :, pl.ds(mine_at, half)].astype(jnp.bfloat16)

    sublane = lax.broadcasted_iota(jnp.int32, (8, LANES), 0)
    top, bottom = sublane == 0, sublane == 7
    lines_all = rows // 8

    def rate(drag, before, centre, after):
        half_v = 0.5 * centre[1]
        up, down = viscosity - half_v, viscosity + half_v
        out = []
        for c in range(3):
            above = pltpu.roll(jnp.where(top, after[c], centre[c]), 7, 0)
            below = pltpu.roll(jnp.where(bottom, before[c], centre[c]), 1, 0)
            out.append(up * above + down * below - drag * centre[c])
        return out

    def fed(change, mean, upstream):
        return [a + mean * b for a, b in zip(change, upstream)]

    def plus(field, factor, change):
        return [u + factor * a for u, a in zip(field, change)]

    def rounded(field):
        return [a.astype(jnp.bfloat16).astype(jnp.float32) for a in field]

    def kept(flag, field):
        return [jnp.where(flag, a, 0.0) for a in field]

    def picked(first, second):
        return [jnp.where(at_inlet, a, b) for a, b in zip(first, second)]

    stage = (time_step * 8.0 / 15.0, time_step * 5.0 / 12.0, time_step * 0.75)
    undo = (-time_step * 17.0 / 60.0, -time_step * 5.0 / 12.0)

    def advance(line_at, lanes, carry, p0, p1, q0, q1):
        means = [params[0, pl.ds(pl.multiple_of(PAD + (line_at - lag) * 8, 8), 8), :] for lag in (1, 2, 3)]
        drags = [mean + 2.0 * viscosity for mean in means]
        first_in = (line_at >= 1) & (line_at <= lines_all)
        second_in = (line_at >= 2) & (line_at <= lines_all + 1)
        (
            p0_b, p0_c, p1_b, p1_c, q0_b, q0_c, q1_b, q1_c,
            q1_s1b, q1_s1c, q1_w1,
            p0_s1b, p0_s1c, p0_w1, p0_s2b, p0_s2c, p0_w2,
            p1_s1b, p1_s1c, p1_w1, p1_s2b, p1_s2c, p1_w2,
        ) = carry

        base0 = plus(q0_c, stage[0], rate(drags[0], q0_b, q0_c, q0))
        f = fed(rate(drags[0], q1_b, q1_c, q1), means[0], q0_c)
        q1_s1a = kept(first_in, plus(q1_c, stage[0], f))
        q1_w1a = plus(q1_s1a, undo[0], f)
        f = fed(rate(drags[0], p0_b, p0_c, p0), means[0], q1_c)
        p0_s1a = kept(first_in, plus(p0_c, stage[0], f))
        p0_w1a = plus(p0_s1a, undo[0], f)
        f = fed(rate(drags[0], p1_b, p1_c, p1), means[0], p0_c)
        p1_s1a = kept(first_in, plus(p1_c, stage[0], f))
        p1_w1a = plus(p1_s1a, undo[0], f)

        base1 = plus(q1_w1, stage[1], rate(drags[1], q1_s1b, q1_s1c, q1_s1a))
        f = fed(rate(drags[1], p0_s1b, p0_s1c, p0_s1a), means[1], picked(q1_b, rounded(q1_s1c)))
        p0_s2a = kept(second_in, plus(p0_w1, stage[1], f))
        p0_w2a = plus(p0_s2a, undo[1], f)
        f = fed(rate(drags[1], p1_s1b, p1_s1c, p1_s1a), means[1], rounded(p0_s1c))
        p1_s2a = kept(second_in, plus(p1_w1, stage[1], f))
        p1_w2a = plus(p1_s2a, undo[1], f)

        base2 = plus(p0_w2, stage[2], rate(drags[2], p0_s2b, p0_s2c, p0_s2a))
        f = fed(rate(drags[2], p1_s2b, p1_s2c, p1_s2a), means[2], rounded(p0_s2c))
        p1_s3 = plus(p1_w2, stage[2], f)

        for lag, values in enumerate((base0, base1, base2)):
            at = pl.ds(pl.multiple_of(PAD + (line_at - lag - 1) * 8, 8), 8)
            for c in range(3):
                base[lag, c, at, lanes] = values[c]

        carry = (
            p0_c, p0, p1_c, p1, q0_c, q0, q1_c, q1,
            q1_s1c, q1_s1a, q1_w1a,
            p0_s1c, p0_s1a, p0_w1a, p0_s2c, p0_s2a, p0_w2a,
            p1_s1c, p1_s1a, p1_w1a, p1_s2c, p1_s2a, p1_w2a,
        )
        return carry, p1_s3

    fields = 23

    def march_block(block, tiles):
        @pl.loop(0, half // LANES)
        def _(column):
            lanes = pl.ds(pl.multiple_of(column * LANES, LANES), LANES)

            def tile_step(i, held):
                tile = block * (STRIDE // TILE_ROWS) + i
                here = rows_of(tile, TILE_ROWS)
                there = rows_of(jnp.maximum(tile - 2, 0), TILE_ROWS)

                def load(ref):
                    values = [ref[c, here, lanes].astype(jnp.float32) for c in range(3)]
                    return [v[0:8] for v in values], [v[8:16] for v in values]

                inputs = [load(own.at[0]), load(own.at[1]), load(behind.at[0]), load(behind.at[1])]
                carry, p1_old = held
                carry, p1_low = advance(2 * tile, lanes, carry, *[value[0] for value in inputs])
                carry, p1_new = advance(2 * tile + 1, lanes, carry, *[value[1] for value in inputs])
                p1_out = [jnp.concatenate([a, b], axis=0).astype(jnp.bfloat16) for a, b in zip(p1_old, p1_low)]

                for c in range(3):
                    done[1, c, there, lanes] = p1_out[c]
                return carry, p1_new

            def restore(at):
                return [state[column, 3 * at + c] for c in range(3)]

            held = tuple(restore(at) for at in range(fields)), restore(fields)
            carry, late = lax.fori_loop(0, tiles, tile_step, held)
            for at, field in enumerate(carry + (late,)):
                for c in range(3):
                    state[column, 3 * at + c] = field[c]

    def finish_block(block):
        @pl.loop(0, half // LANES)
        def _(column):
            lanes = pl.ds(pl.multiple_of(column * LANES, LANES), LANES)

            @pl.loop(0, FINE // TILE_ROWS)
            def _(i):
                tile = block * (FINE // TILE_ROWS) + i
                here = rows_of(tile, TILE_ROWS)
                there = pl.ds(pl.multiple_of(PAD + tile * TILE_ROWS, TILE_ROWS), TILE_ROWS)
                mean = params[0, there, :]
                r1 = [far[c, here, lanes].astype(jnp.float32) for c in range(3)]
                q1 = [behind[1, c, here, lanes].astype(jnp.float32) for c in range(3)]
                held = [[base[k, c, there, lanes] for c in range(3)] for k in range(3)]
                q0_s1 = rounded(plus(held[0], stage[0] * mean, r1))
                q1_s2 = picked(q1, rounded(plus(held[1], stage[1] * mean, q0_s1)))
                p0_out = [a.astype(jnp.bfloat16) for a in plus(held[2], stage[2] * mean, q1_s2)]

                for c in range(3):
                    done[0, c, here, lanes] = p0_out[c]

    pieces = STRIDE // PIECE

    @pl.loop(0, blocks + 1)
    def _(block):
        @pl.when(block < blocks)
        def _():
            start_far(block)

        march_block(block, jnp.where(block < blocks, STRIDE // TILE_ROWS, PAD // TILE_ROWS))

        @pl.when(block >= 1)
        def _():
            leave(1, rows_of(block * pieces - 1, PIECE))

        @pl.when(block < blocks)
        def _():
            for piece in range(pieces - 1):
                leave(1, rows_of(block * pieces + piece, PIECE))

    @pl.loop(0, rows // FINE)
    def _(block):
        @pl.when(gets_far)
        def _():
            far_copy(block).wait_recv()

        finish_block(block)
        leave(0, rows_of(block, FINE))

    other_copy(0, every).wait_send()

    @pl.when(has_after)
    def _():
        near_copy(0, every).wait_send()

        @pl.when(parity == 0)
        def _():
            further_copy(0, every).wait_send()
            for block in range(crossing):
                across_copy(block).wait_send()

        @pl.when(parity == 1)
        def _():
            further_copy(0, pl.ds(crossing * STRIDE, rows - crossing * STRIDE)).wait_send()

    @pl.when(gives_far)
    def _():
        far_copy(0, every).wait_send()

    own_copy(parity, every).wait()
    back_copy(every).wait_send()
    back_copy(every).wait_recv()


def leave_kernel(next_ref, flow_ref, next_out, flow_out, sem):
    copies = []
    for c in range(3):
        copies.append(pltpu.make_async_copy(flow_ref.at[c], flow_out.at[c], sem.at[c]))
        copies.append(pltpu.make_async_copy(next_ref.at[c], next_out.at[c], sem.at[3 + c]))
    for copy in copies:
        copy.start()
    for copy in copies:
        copy.wait()


def body(velocity, mean_flow, chol_diag, chol_off, eddy_x, eddy_y, eddy_z, eddy_signs, tile_lists):
    rows, columns = velocity.shape[2:]
    count = lax.axis_size("yz")
    slabs = lax.axis_size("gx")
    eddies = eddy_x.shape[0]
    blocks = rows // STRIDE
    cosine, low, sine = wall_bases(rows)
    table = mode_table(rows, columns, count)
    given = [
        velocity[:, 0], jnp.asarray(cosine), jnp.asarray(low), jnp.asarray(sine),
        mean_flow, chol_diag, chol_off, eddy_x, eddy_y, eddy_z, eddy_signs, jnp.asarray(table),
    ]
    small = [pltpu.VMEM(value.shape, value.dtype) for value in given[4:]]
    given = [pltpu.with_memory_space_constraint(value, pltpu.HBM) for value in given]
    vmem = pl.BlockSpec(memory_space=pltpu.VMEM)
    hbm = pl.BlockSpec(memory_space=pl.ANY)
    half = columns // 2
    pair = pltpu.VMEM((2, 3, rows + PAD, half), jnp.bfloat16)
    square = pltpu.VMEM((rows, rows), jnp.bfloat16)
    lines = pltpu.VMEM((columns, rows), jnp.float32)
    lines16 = pltpu.VMEM((columns, rows), jnp.bfloat16)
    velocity_next, inflow = pl.pallas_call(
        functools.partial(step_kernel, slabs, count),
        out_shape=[
            pltpu.VMEM((3, rows, columns), jnp.bfloat16),
            pltpu.VMEM((3, rows, columns), jnp.float32),
        ],
        in_specs=[hbm] * len(given),
        out_specs=[vmem, vmem],
        scratch_shapes=small
        + [
            pair,
            pair,
            pltpu.VMEM((3, rows + PAD, half), jnp.bfloat16),
            pltpu.VMEM((2, 3, rows, half), jnp.bfloat16),
            pltpu.VMEM((half // LANES, 3 * 24, 8, LANES), jnp.float32),
            pltpu.VMEM((3, 3, rows + 2 * PAD, half), jnp.float32),
        ]
        + [square] * 3
        + [
            pltpu.VMEM((7, rows + 2 * PAD, LANES), jnp.float32),
            pltpu.VMEM((3, columns, eddies), jnp.bfloat16),
            pltpu.VMEM((3, 16, eddies), jnp.bfloat16),
            pltpu.VMEM((8, columns), jnp.float32),
            lines16, lines16, lines, lines, lines, lines16, lines16,
            pltpu.VMEM((count, 8, rows), jnp.float32),
            pltpu.SemaphoreType.DMA((12,)),
        ]
        + [pltpu.SemaphoreType.DMA(()), pltpu.SemaphoreType.DMA((blocks,))] * 3
        + [pltpu.SemaphoreType.DMA(()), pltpu.SemaphoreType.DMA((rows // FINE,))]
        + [pltpu.SemaphoreType.DMA(())] * 4
        + [pltpu.SemaphoreType.DMA((count - 1,))] * 2,
        compiler_params=pltpu.CompilerParams(
            collective_id=0, has_side_effects=True, vmem_limit_bytes=52 * 1024 * 1024
        ),
        cost_estimate=pl.CostEstimate(
            flops=2 * rows * columns * (3 * eddies + 5 * rows), bytes_accessed=24 * rows * columns, transcendentals=0
        ),
        name="step",
    )(*given)
    velocity_next, inflow = pl.pallas_call(
        leave_kernel,
        out_shape=[
            jax.ShapeDtypeStruct(velocity_next.shape, jnp.bfloat16),
            jax.ShapeDtypeStruct(inflow.shape, jnp.float32),
        ],
        in_specs=[vmem, vmem],
        out_specs=[hbm, hbm],
        scratch_shapes=[pltpu.SemaphoreType.DMA((6,))],
        compiler_params=pltpu.CompilerParams(vmem_limit_bytes=1024 * 1024),
        cost_estimate=pl.CostEstimate(flops=0, bytes_accessed=36 * rows * columns, transcendentals=0),
        name="leave",
    )(*(pltpu.with_memory_space_constraint(value, pltpu.VMEM) for value in (velocity_next, inflow)))
    return velocity_next[:, None], inflow[None]


def solution(mesh):
    placed = (P(None, "gx", None, "yz"), P(), P(), P(), P(), P(), P(), P(), P("yz", None))
    return jax.shard_map(
        body,
        mesh=mesh,
        in_specs=placed,
        out_specs=(P(None, "gx", None, "yz"), P(None, None, None, "yz")),
        check_vma=False,
    )
```

```python
import functools
import math

import jax
import jax.numpy as jnp
import numpy as np
from jax import lax
from jax.experimental import pallas as pl
from jax.experimental.pallas import tpu as pltpu
from jax.sharding import PartitionSpec as P

TILE = 128
EPT = 96
SIGMA = 64
LANES = 128
STRIDE = 64
PIECE = 32
FINE = 32
TILE_ROWS = 16
PAD = 32
BAND = 256
MESH = pl.DeviceIdType.MESH

shape_peak = math.sqrt(1.5)
time_step = 0.4
viscosity = 0.3

THETA, RATE, RATE2, RATE4, ALPHA, BETA, PERIOD, POWERS = range(8)


def tent_shape(ratio):
    return shape_peak * jnp.maximum(0.0, 1.0 - jnp.abs(ratio))


def wall_bases(rows):
    k = np.arange(rows)[None, :]
    y = np.arange(rows)[:, None]
    norm = np.where(k == 0, math.sqrt(1.0 / rows), math.sqrt(2.0 / rows))
    cosine = norm * np.cos((k * (2 * y + 1) % (4 * rows)) * (math.pi / (2 * rows)))
    sine = math.sqrt(2.0 / rows) * np.sin((k * (y + 1) % (2 * rows)) * (math.pi / rows))
    high = cosine.astype(jnp.bfloat16)
    low = (cosine - high.astype(np.float64)).astype(jnp.bfloat16)
    return high, low, sine.astype(jnp.bfloat16)


def mode_table(rows, length, count):
    theta = 2.0 * np.arcsinh(np.sin(np.arange(rows) * (math.pi / (2 * rows))))
    rate = np.exp(-theta)
    period = np.where(theta > 0, 1.0 / np.maximum(-np.expm1(-theta * length * count), 1e-30), 1.0)
    table = [theta, rate, rate**2, rate**4, rate / (1.0 + rate), np.sqrt(rate) / (1.0 + rate), period]
    table += [np.exp(-theta * length * q) for q in range(count)]
    table += [np.zeros(rows)] * (-len(table) % 8)
    return np.stack(table).astype(np.float32)


def dot(a, b, contract):
    return lax.dot_general(a, b, (contract, ((), ())), preferred_element_type=jnp.float32)


NN = ((1,), (0,))
NT = ((1,), (1,))


def step_kernel(
    slabs, count,
    vel_ref, cos_hbm, low_hbm, sin_hbm, mean_hbm, diag_hbm, off_hbm, x_hbm, y_hbm, z_hbm, sign_hbm, table_hbm,
    next_ref, flow_ref,
    mean_ref, diag_ref, off_ref, x_ref, y_ref, z_ref, sign_ref, table_ref,
    own, behind, far, done, state, base,
    cosine, cosine_low, sine, params, weight, edge_weight, carry_row,
    div_high, div_low, modes, ups, downs, slope_modes, rise_modes, sums,
    load_sem, other_send, other_recv, near_send, near_recv, further_send, further_recv,
    far_send, far_recv, across_send, back_send, back_recv, own_sem, sum_send, sum_recv,
):
    rows, columns = flow_ref.shape[1:]
    half = columns // 2
    spanwise = columns * count
    eddies = sign_ref.shape[1]
    blocks = rows // STRIDE
    me = lax.axis_index("gx")
    pencil = lax.axis_index("yz")
    parity = lax.rem(me, 2)
    partner = me + 1 - 2 * parity
    has_after = me + 2 < slabs
    has_before = me >= 2
    gets_far = me >= 4
    gives_far = has_after & (me >= 2)
    gives_across = has_after & (parity == 0)
    across = jnp.where(has_after, me + 3, me - 1)
    after = jnp.where(has_after, me + 2, me - 2)
    at_inlet = me < 2
    after_inlet = (me >= 2) & (me < 4)
    mine_at = pl.multiple_of(parity * half, half)
    theirs_at = pl.multiple_of((1 - parity) * half, half)

    barrier = pltpu.get_barrier_semaphore()
    pl.semaphore_signal(barrier, inc=1, device_id={"gx": partner}, device_id_type=MESH)
    for step in range(1, count):
        pl.semaphore_signal(barrier, inc=1, device_id={"yz": lax.rem(pencil + step, count)}, device_id_type=MESH)

    @pl.when(has_after)
    def _():
        pl.semaphore_signal(barrier, inc=1, device_id={"gx": after}, device_id_type=MESH)

    @pl.when(has_before)
    def _():
        pl.semaphore_signal(barrier, inc=1, device_id={"gx": me - 2}, device_id_type=MESH)

    @pl.when(has_before & (parity == 1))
    def _():
        pl.semaphore_signal(barrier, inc=1, device_id={"gx": me - 3}, device_id_type=MESH)

    loads = [
        pltpu.make_async_copy(
            vel_ref.at[:, :, pl.ds(mine_at, half)], own.at[parity, :, pl.ds(0, rows), :], load_sem.at[0]
        ),
        pltpu.make_async_copy(cos_hbm, cosine, load_sem.at[1]),
        pltpu.make_async_copy(low_hbm, cosine_low, load_sem.at[2]),
        pltpu.make_async_copy(sin_hbm, sine, load_sem.at[3]),
    ]
    small = [
        pltpu.make_async_copy(source, target, load_sem.at[4 + at])
        for at, (source, target) in enumerate(
            [
                (mean_hbm, mean_ref), (diag_hbm, diag_ref), (off_hbm, off_ref), (x_hbm, x_ref),
                (y_hbm, y_ref), (z_hbm, z_ref), (sign_hbm, sign_ref), (table_hbm, table_ref),
            ]
        )
    ]

    pl.semaphore_wait(
        barrier,
        count + has_after.astype(jnp.int32) + has_before.astype(jnp.int32) + gives_across.astype(jnp.int32),
    )

    def rows_of(block, size=STRIDE):
        return pl.ds(pl.multiple_of(block * size, size), size)

    def send(source, target, send_sem, recv_sem, device):
        return pltpu.make_async_remote_copy(
            src_ref=source,
            dst_ref=target,
            send_sem=send_sem,
            recv_sem=recv_sem,
            device_id={"gx": device},
            device_id_type=MESH,
        )

    every = pl.ds(0, rows)

    def other_copy(block, here=None):
        here = rows_of(block) if here is None else here
        source = vel_ref.at[:, here, pl.ds(theirs_at, half)]
        return send(source, own.at[parity, :, here, :], other_send, other_recv.at[block], partner)

    def near_copy(block, here=None):
        here = rows_of(block) if here is None else here
        source = vel_ref.at[:, here, pl.ds(mine_at, half)]
        return send(source, behind.at[parity, :, here, :], near_send, near_recv.at[block], after)

    def further_copy(block, here=None):
        here = rows_of(block) if here is None else here
        source, target = own.at[1 - parity, :, here, :], behind.at[1 - parity, :, here, :]
        return send(source, target, further_send, further_recv.at[block], after)

    def across_copy(block):
        here = rows_of(block)
        source, target = vel_ref.at[:, here, pl.ds(theirs_at, half)], behind.at[parity, :, here, :]
        return send(source, target, across_send, further_recv.at[block], across)

    def far_copy(block, here=None):
        here = rows_of(block, FINE) if here is None else here
        return send(behind.at[1, :, here, :], far.at[:, here, :], far_send, far_recv.at[block], after)

    def back_copy(here):
        target = next_ref.at[:, here, pl.ds(mine_at, half)]
        return send(done.at[1 - parity, :, here, :], target, back_send, back_recv, partner)

    def own_copy(plane, here):
        return pltpu.make_async_copy(
            done.at[plane, :, here, :], next_ref.at[:, here, pl.ds(mine_at, half)], own_sem
        )

    def leave(plane, here):
        @pl.when(parity == plane)
        def _():
            own_copy(plane, here).start()

        @pl.when(parity != plane)
        def _():
            back_copy(here).start()

    @pl.loop(0, blocks)
    def _(block):
        @pl.when(has_after)
        def _():
            near_copy(block).start()

        other_copy(block).start()

    for load in small + loads:
        load.start()

    crossing = 1

    @pl.when(gives_across)
    def _():
        for block in range(crossing):
            across_copy(block).start()

    def start_further(block):
        other_copy(block).wait_recv()

        @pl.when(has_after & ((parity == 0) | (block >= crossing)))
        def _():
            further_copy(block).start()

    def start_far(block):
        @pl.when(has_before)
        def _():
            near_copy(block).wait_recv()
            further_copy(block).wait_recv()

        @pl.when(gives_far)
        def _():
            for part in range(STRIDE // FINE):
                far_copy(block * (STRIDE // FINE) + part).start()

    beyond = pl.ds(rows, PAD)
    own[:, :, beyond, :] = jnp.zeros((2, 3, PAD, half), jnp.bfloat16)
    behind[:, :, beyond, :] = jnp.zeros((2, 3, PAD, half), jnp.bfloat16)
    far[:, beyond, :] = jnp.zeros((3, PAD, half), jnp.bfloat16)
    state[...] = jnp.zeros_like(state)

    @pl.when(at_inlet)
    def _():
        behind[0] = jnp.zeros_like(behind[0])
        far[...] = jnp.zeros_like(far)

    for load in small:
        load.wait()

    for edge in (0, PAD + rows):
        params[0, pl.ds(edge, PAD), :] = jnp.zeros((PAD, LANES), jnp.float32)
    for place, row in enumerate(
        [mean_ref[...].reshape(1, rows)] + [diag_ref[c : c + 1, :] for c in range(3)] + [off_ref[c : c + 1, :] for c in range(3)]
    ):
        params[place, pl.ds(PAD, rows), :] = jnp.transpose(jnp.broadcast_to(row, (LANES, rows)))

    first_cell = pencil * columns
    amplitude = math.sqrt(8.0 * rows / (TILE * EPT))
    eddy_x, eddy_y, eddy_z = (ref[...].reshape(1, eddies) for ref in (x_ref, y_ref, z_ref))
    stretch = amplitude * tent_shape(eddy_x.astype(jnp.float32) / SIGMA)
    scales = [stretch * (2 * sign_ref[j : j + 1, :] - 1).astype(jnp.float32) for j in range(3)]

    def weights(start, extent):
        cells = start + lax.broadcasted_iota(jnp.int32, (extent, eddies), 0)
        offset = cells - eddy_z
        offset = jnp.where(offset >= spanwise // 2, offset - spanwise, offset)
        offset = jnp.where(offset < -(spanwise // 2), offset + spanwise, offset)
        shape_z = tent_shape(offset.astype(jnp.float32) / SIGMA)
        return [(scale * shape_z).astype(jnp.bfloat16) for scale in scales]

    @pl.loop(0, columns // LANES)
    def _(tile):
        start = pl.multiple_of(tile * LANES, LANES)
        for j, value in enumerate(weights(first_cell + start, LANES)):
            weight[j, pl.ds(start, LANES), :] = value

    for j, value in enumerate(weights(jnp.where(pencil == 0, spanwise, first_cell) - 1, 16)):
        edge_weight[j] = value

    carry_row[...] = jnp.zeros_like(carry_row)

    @pl.loop(0, rows // BAND)
    def _(band):
        start = pl.multiple_of(band * BAND, BAND)
        here = pl.ds(start, BAND)
        cells = start + lax.broadcasted_iota(jnp.int32, (BAND, eddies), 0)
        shape_y = tent_shape((cells - eddy_y).astype(jnp.float32) / SIGMA).astype(jnp.bfloat16)
        fl = [dot(shape_y, weight[j], NT) for j in range(3)]
        ends = [dot(shape_y, edge_weight[j], NT)[:, 0:1] for j in range(3)]

        def spread(place):
            return jnp.concatenate([params[place, pl.ds(PAD + start, BAND), :]] * (columns // LANES), axis=1)

        flow_ref[0, here, :] = spread(0) + spread(1) * fl[0]
        row = start + lax.broadcasted_iota(jnp.int32, (BAND, columns), 0)
        flux = jnp.where(row == rows - 1, 0.0, spread(4) * fl[0] + spread(2) * fl[1])
        third = spread(5) * fl[0] + spread(6) * fl[1] + spread(3) * fl[2]
        edge = (
            params[5, pl.ds(PAD + start, BAND), 0:1] * ends[0] + params[6, pl.ds(PAD + start, BAND), 0:1] * ends[1] + params[3, pl.ds(PAD + start, BAND), 0:1] * ends[2]
        )
        lower = jnp.where(row == start, carry_row[0:1, :], pltpu.roll(flux, 1, 0))
        lane = lax.broadcasted_iota(jnp.int32, (BAND, columns), 1)
        previous = jnp.where(lane == 0, edge, pltpu.roll(third, 1, 1))
        carry_row[0:1, :] = flux[BAND - 1 : BAND, :]
        flow_ref[1, here, :] = flux
        flow_ref[2, here, :] = third
        div = jnp.transpose(flux - lower + third - previous)
        high = div.astype(jnp.bfloat16)
        div_high[:, here] = high
        div_low[:, here] = (div - high.astype(jnp.float32)).astype(jnp.bfloat16)

    loads[1].wait()
    loads[2].wait()

    @pl.loop(0, rows // BAND)
    def _(band):
        here = pl.ds(pl.multiple_of(band * BAND, BAND), BAND)
        wall = cosine[:, here]
        modes[:, here] = (
            dot(div_high[...], wall, NN) + dot(div_low[...], wall, NN) + dot(div_high[...], cosine_low[:, here], NN)
        )

    def entry(place):
        return table_ref[place : place + 1, :]

    line = lax.broadcasted_iota(jnp.int32, (8, rows), 0)
    line_f = line.astype(jnp.float32)
    theta, rate, rate2, rate4 = entry(THETA), entry(RATE), entry(RATE2), entry(RATE4)
    steps = columns // 8

    def scan_step(step, carry):
        up_carry, down_carry, run = carry
        at = pl.ds(pl.multiple_of(step * 8, 8), 8)
        value = modes[at, :]
        value = value + jnp.where(line >= 1, rate, 0.0) * pltpu.roll(value, 1, 0)
        value = value + jnp.where(line >= 2, rate2, 0.0) * pltpu.roll(value, 2, 0)
        value = value + jnp.where(line >= 4, rate4, 0.0) * pltpu.roll(value, 4, 0)
        value = value + jnp.exp(-theta * (line_f + 1.0)) * up_carry
        ups[at, :] = value
        at = pl.ds(pl.multiple_of((steps - 1 - step) * 8, 8), 8)
        down = modes[at, :]
        down = down + jnp.where(line < 7, rate, 0.0) * pltpu.roll(down, 7, 0)
        down = down + jnp.where(line < 6, rate2, 0.0) * pltpu.roll(down, 6, 0)
        down = down + jnp.where(line < 4, rate4, 0.0) * pltpu.roll(down, 4, 0)
        down = down + jnp.exp(-theta * (8.0 - line_f)) * down_carry
        downs[at, :] = jnp.where(line == 7, down_carry, pltpu.roll(down, 7, 0))
        return value[7:8, :], down[0:1, :], run + value

    zeros = jnp.zeros((1, rows), jnp.float32)
    sum_up, sum_down, run = lax.fori_loop(0, steps, scan_step, (zeros, zeros, jnp.zeros((8, rows), jnp.float32)))
    run = jnp.sum(run, axis=0, keepdims=True)
    sums[pencil] = jnp.where(line == 0, sum_up, jnp.where(line == 1, sum_down, run))

    def sum_copy(step):
        return pltpu.make_async_remote_copy(
            src_ref=sums.at[pencil],
            dst_ref=sums.at[pencil],
            send_sem=sum_send.at[step - 1],
            recv_sem=sum_recv.at[step - 1],
            device_id={"yz": lax.rem(pencil + step, count)},
            device_id_type=MESH,
        )

    for step in range(1, count):
        sum_copy(step).start()
    for step in range(1, count):
        sum_copy(step).wait_send()
        sum_copy(step).wait_recv()

    total_cells = float(spanwise)
    mean = sum(sums[p, 0:1, :] for p in range(count)) / total_cells
    carry_up, carry_down = zeros, zeros
    start, mine, before, shift = zeros, zeros, zeros, zeros
    for p in range(count):
        hops_up = lax.rem(pencil - 1 - p + 2 * count, count)
        hops_down = lax.rem(p - pencil - 1 + count, count)
        carry_up = carry_up + table_ref[pl.ds(POWERS + hops_up, 1), :] * sums[p, 0:1, :]
        carry_down = carry_down + table_ref[pl.ds(POWERS + hops_down, 1), :] * sums[p, 1:2, :]
        total = sums[p, 0:1, :] - mean * columns
        start = start + jnp.where(pencil == p, before, 0.0)
        mine = mine + jnp.where(pencil == p, total, 0.0)
        shift = shift + sums[p, 2:3, :] - mean * (columns * (columns + 1) / 2.0) + columns * before
        before = before + total
    start = start - shift / total_cells
    first = lax.broadcasted_iota(jnp.int32, (1, rows), 1) == 0
    carry_up = jnp.where(first, start, entry(PERIOD) * carry_up)
    carry_down = jnp.where(first, -start - mine, entry(PERIOD) * carry_down)
    mean = jnp.where(first, mean, 0.0)
    alpha, beta = entry(ALPHA), entry(BETA)

    @pl.loop(0, steps // 2)
    def _(step):
        slopes, rises = [], []
        for part in range(2):
            at = pl.ds(pl.multiple_of(step * 16 + part * 8, 8), 8)
            up_count = line_f + (step * 16 + part * 8 + 1).astype(jnp.float32)
            down_count = columns - up_count
            up = ups[at, :] + jnp.exp(-theta * up_count) * carry_up - mean * up_count
            down = downs[at, :] + jnp.exp(-theta * down_count) * carry_down - mean * down_count
            slopes.append(alpha * (up - down))
            rises.append(beta * (up + rate * down))
        at = pl.ds(pl.multiple_of(step * 16, 16), 16)
        slope_modes[at, :] = jnp.concatenate(slopes, axis=0).astype(jnp.bfloat16)
        rise_modes[at, :] = jnp.concatenate(rises, axis=0).astype(jnp.bfloat16)

    @pl.loop(0, blocks)
    def _(block):
        start_further(block)

    loads[3].wait()

    @pl.loop(0, rows // BAND)
    def _(band):
        here = pl.ds(pl.multiple_of(band * BAND, BAND), BAND)
        flow_ref[2, here, :] = flow_ref[2, here, :] - dot(cosine[here, :], slope_modes[...], NT)
        flow_ref[1, here, :] = flow_ref[1, here, :] - dot(sine[here, :], rise_modes[...], NT)

    loads[0].wait()

    @pl.when(at_inlet)
    def _():
        behind[1, :, pl.ds(0, rows), :] = flow_ref[:, :, pl.ds(mine_at, half)].astype(jnp.bfloat16)

    @pl.when(after_inlet)
    def _():
        far[:, pl.ds(0, rows), :] = flow_ref[:, :, pl.ds(mine_at, half)].astype(jnp.bfloat16)

    sublane = lax.broadcasted_iota(jnp.int32, (8, LANES), 0)
    top, bottom = sublane == 0, sublane == 7
    lines_all = rows // 8

    def rate(drag, before, centre, after):
        half_v = 0.5 * centre[1]
        up, down = viscosity - half_v, viscosity + half_v
        out = []
        for c in range(3):
            above = pltpu.roll(jnp.where(top, after[c], centre[c]), 7, 0)
            below = pltpu.roll(jnp.where(bottom, before[c], centre[c]), 1, 0)
            out.append(up * above + down * below - drag * centre[c])
        return out

    def fed(change, mean, upstream):
        return [a + mean * b for a, b in zip(change, upstream)]

    def plus(field, factor, change):
        return [u + factor * a for u, a in zip(field, change)]

    def rounded(field):
        return [a.astype(jnp.bfloat16).astype(jnp.float32) for a in field]

    def kept(flag, field):
        return [jnp.where(flag, a, 0.0) for a in field]

    def picked(first, second):
        return [jnp.where(at_inlet, a, b) for a, b in zip(first, second)]

    stage = (time_step * 8.0 / 15.0, time_step * 5.0 / 12.0, time_step * 0.75)
    undo = (-time_step * 17.0 / 60.0, -time_step * 5.0 / 12.0)

    def advance(line_at, lanes, carry, p0, p1, q0, q1):
        means = [params[0, pl.ds(pl.multiple_of(PAD + (line_at - lag) * 8, 8), 8), :] for lag in (1, 2, 3)]
        drags = [mean + 2.0 * viscosity for mean in means]
        first_in = (line_at >= 1) & (line_at <= lines_all)
        second_in = (line_at >= 2) & (line_at <= lines_all + 1)
        (
            p0_b, p0_c, p1_b, p1_c, q0_b, q0_c, q1_b, q1_c,
            q1_s1b, q1_s1c, q1_w1,
            p0_s1b, p0_s1c, p0_w1, p0_s2b, p0_s2c, p0_w2,
            p1_s1b, p1_s1c, p1_w1, p1_s2b, p1_s2c, p1_w2,
        ) = carry

        base0 = plus(q0_c, stage[0], rate(drags[0], q0_b, q0_c, q0))
        f = fed(rate(drags[0], q1_b, q1_c, q1), means[0], q0_c)
        q1_s1a = kept(first_in, plus(q1_c, stage[0], f))
        q1_w1a = plus(q1_s1a, undo[0], f)
        f = fed(rate(drags[0], p0_b, p0_c, p0), means[0], q1_c)
        p0_s1a = kept(first_in, plus(p0_c, stage[0], f))
        p0_w1a = plus(p0_s1a, undo[0], f)
        f = fed(rate(drags[0], p1_b, p1_c, p1), means[0], p0_c)
        p1_s1a = kept(first_in, plus(p1_c, stage[0], f))
        p1_w1a = plus(p1_s1a, undo[0], f)

        base1 = plus(q1_w1, stage[1], rate(drags[1], q1_s1b, q1_s1c, q1_s1a))
        f = fed(rate(drags[1], p0_s1b, p0_s1c, p0_s1a), means[1], picked(q1_b, rounded(q1_s1c)))
        p0_s2a = kept(second_in, plus(p0_w1, stage[1], f))
        p0_w2a = plus(p0_s2a, undo[1], f)
        f = fed(rate(drags[1], p1_s1b, p1_s1c, p1_s1a), means[1], rounded(p0_s1c))
        p1_s2a = kept(second_in, plus(p1_w1, stage[1], f))
        p1_w2a = plus(p1_s2a, undo[1], f)

        base2 = plus(p0_w2, stage[2], rate(drags[2], p0_s2b, p0_s2c, p0_s2a))
        f = fed(rate(drags[2], p1_s2b, p1_s2c, p1_s2a), means[2], rounded(p0_s2c))
        p1_s3 = plus(p1_w2, stage[2], f)

        for lag, values in enumerate((base0, base1, base2)):
            at = pl.ds(pl.multiple_of(PAD + (line_at - lag - 1) * 8, 8), 8)
            for c in range(3):
                base[lag, c, at, lanes] = values[c]

        carry = (
            p0_c, p0, p1_c, p1, q0_c, q0, q1_c, q1,
            q1_s1c, q1_s1a, q1_w1a,
            p0_s1c, p0_s1a, p0_w1a, p0_s2c, p0_s2a, p0_w2a,
            p1_s1c, p1_s1a, p1_w1a, p1_s2c, p1_s2a, p1_w2a,
        )
        return carry, p1_s3

    fields = 23

    def march_block(block, tiles):
        @pl.loop(0, half // LANES)
        def _(column):
            lanes = pl.ds(pl.multiple_of(column * LANES, LANES), LANES)

            def tile_step(i, held):
                tile = block * (STRIDE // TILE_ROWS) + i
                here = rows_of(tile, TILE_ROWS)
                there = rows_of(jnp.maximum(tile - 2, 0), TILE_ROWS)

                def load(ref):
                    values = [ref[c, here, lanes].astype(jnp.float32) for c in range(3)]
                    return [v[0:8] for v in values], [v[8:16] for v in values]

                inputs = [load(own.at[0]), load(own.at[1]), load(behind.at[0]), load(behind.at[1])]
                carry, p1_old = held
                carry, p1_low = advance(2 * tile, lanes, carry, *[value[0] for value in inputs])
                carry, p1_new = advance(2 * tile + 1, lanes, carry, *[value[1] for value in inputs])
                p1_out = [jnp.concatenate([a, b], axis=0).astype(jnp.bfloat16) for a, b in zip(p1_old, p1_low)]

                for c in range(3):
                    done[1, c, there, lanes] = p1_out[c]
                return carry, p1_new

            def restore(at):
                return [state[column, 3 * at + c] for c in range(3)]

            held = tuple(restore(at) for at in range(fields)), restore(fields)
            carry, late = lax.fori_loop(0, tiles, tile_step, held)
            for at, field in enumerate(carry + (late,)):
                for c in range(3):
                    state[column, 3 * at + c] = field[c]

    def finish_block(block):
        @pl.loop(0, half // LANES)
        def _(column):
            lanes = pl.ds(pl.multiple_of(column * LANES, LANES), LANES)

            @pl.loop(0, FINE // TILE_ROWS)
            def _(i):
                tile = block * (FINE // TILE_ROWS) + i
                here = rows_of(tile, TILE_ROWS)
                there = pl.ds(pl.multiple_of(PAD + tile * TILE_ROWS, TILE_ROWS), TILE_ROWS)
                mean = params[0, there, :]
                r1 = [far[c, here, lanes].astype(jnp.float32) for c in range(3)]
                q1 = [behind[1, c, here, lanes].astype(jnp.float32) for c in range(3)]
                held = [[base[k, c, there, lanes] for c in range(3)] for k in range(3)]
                q0_s1 = rounded(plus(held[0], stage[0] * mean, r1))
                q1_s2 = picked(q1, rounded(plus(held[1], stage[1] * mean, q0_s1)))
                p0_out = [a.astype(jnp.bfloat16) for a in plus(held[2], stage[2] * mean, q1_s2)]

                for c in range(3):
                    done[0, c, here, lanes] = p0_out[c]

    pieces = STRIDE // PIECE

    @pl.loop(0, blocks + 1)
    def _(block):
        @pl.when(block < blocks)
        def _():
            start_far(block)

        march_block(block, jnp.where(block < blocks, STRIDE // TILE_ROWS, PAD // TILE_ROWS))

        @pl.when(block >= 1)
        def _():
            leave(1, rows_of(block * pieces - 1, PIECE))

        @pl.when(block < blocks)
        def _():
            for piece in range(pieces - 1):
                leave(1, rows_of(block * pieces + piece, PIECE))

    @pl.loop(0, rows // FINE)
    def _(block):
        @pl.when(gets_far)
        def _():
            far_copy(block).wait_recv()

        finish_block(block)
        leave(0, rows_of(block, FINE))

    other_copy(0, every).wait_send()

    @pl.when(has_after)
    def _():
        near_copy(0, every).wait_send()

        @pl.when(parity == 0)
        def _():
            further_copy(0, every).wait_send()
            for block in range(crossing):
                across_copy(block).wait_send()

        @pl.when(parity == 1)
        def _():
            further_copy(0, pl.ds(crossing * STRIDE, rows - crossing * STRIDE)).wait_send()

    @pl.when(gives_far)
    def _():
        far_copy(0, every).wait_send()

    own_copy(parity, every).wait()
    back_copy(every).wait_send()
    back_copy(every).wait_recv()


def leave_kernel(next_ref, flow_ref, next_out, flow_out, sem):
    copies = []
    for c in range(3):
        copies.append(pltpu.make_async_copy(flow_ref.at[c], flow_out.at[c], sem.at[c]))
        copies.append(pltpu.make_async_copy(next_ref.at[c], next_out.at[c], sem.at[3 + c]))
    for copy in copies:
        copy.start()
    for copy in copies:
        copy.wait()


def body(velocity, mean_flow, chol_diag, chol_off, eddy_x, eddy_y, eddy_z, eddy_signs, tile_lists):
    rows, columns = velocity.shape[2:]
    count = lax.axis_size("yz")
    slabs = lax.axis_size("gx")
    eddies = eddy_x.shape[0]
    blocks = rows // STRIDE
    cosine, low, sine = wall_bases(rows)
    table = mode_table(rows, columns, count)
    given = [
        velocity[:, 0], jnp.asarray(cosine), jnp.asarray(low), jnp.asarray(sine),
        mean_flow, chol_diag, chol_off, eddy_x, eddy_y, eddy_z, eddy_signs, jnp.asarray(table),
    ]
    small = [pltpu.VMEM(value.shape, value.dtype) for value in given[4:]]
    given = [pltpu.with_memory_space_constraint(value, pltpu.HBM) for value in given]
    vmem = pl.BlockSpec(memory_space=pltpu.VMEM)
    hbm = pl.BlockSpec(memory_space=pl.ANY)
    half = columns // 2
    pair = pltpu.VMEM((2, 3, rows + PAD, half), jnp.bfloat16)
    square = pltpu.VMEM((rows, rows), jnp.bfloat16)
    lines = pltpu.VMEM((columns, rows), jnp.float32)
    lines16 = pltpu.VMEM((columns, rows), jnp.bfloat16)
    velocity_next, inflow = pl.pallas_call(
        functools.partial(step_kernel, slabs, count),
        out_shape=[
            pltpu.VMEM((3, rows, columns), jnp.bfloat16),
            pltpu.VMEM((3, rows, columns), jnp.float32),
        ],
        in_specs=[hbm] * len(given),
        out_specs=[vmem, vmem],
        scratch_shapes=small
        + [
            pair,
            pair,
            pltpu.VMEM((3, rows + PAD, half), jnp.bfloat16),
            pltpu.VMEM((2, 3, rows, half), jnp.bfloat16),
            pltpu.VMEM((half // LANES, 3 * 24, 8, LANES), jnp.float32),
            pltpu.VMEM((3, 3, rows + 2 * PAD, half), jnp.float32),
        ]
        + [square] * 3
        + [
            pltpu.VMEM((7, rows + 2 * PAD, LANES), jnp.float32),
            pltpu.VMEM((3, columns, eddies), jnp.bfloat16),
            pltpu.VMEM((3, 16, eddies), jnp.bfloat16),
            pltpu.VMEM((8, columns), jnp.float32),
            lines16, lines16, lines, lines, lines, lines16, lines16,
            pltpu.VMEM((count, 8, rows), jnp.float32),
            pltpu.SemaphoreType.DMA((12,)),
        ]
        + [pltpu.SemaphoreType.DMA(()), pltpu.SemaphoreType.DMA((blocks,))] * 3
        + [pltpu.SemaphoreType.DMA(()), pltpu.SemaphoreType.DMA((rows // FINE,))]
        + [pltpu.SemaphoreType.DMA(())] * 4
        + [pltpu.SemaphoreType.DMA((count - 1,))] * 2,
        compiler_params=pltpu.CompilerParams(
            collective_id=0, has_side_effects=True, vmem_limit_bytes=52 * 1024 * 1024
        ),
        cost_estimate=pl.CostEstimate(
            flops=2 * rows * columns * (3 * eddies + 5 * rows), bytes_accessed=24 * rows * columns, transcendentals=0
        ),
        name="step",
    )(*given)
    velocity_next, inflow = pl.pallas_call(
        leave_kernel,
        out_shape=[
            jax.ShapeDtypeStruct(velocity_next.shape, jnp.bfloat16),
            jax.ShapeDtypeStruct(inflow.shape, jnp.float32),
        ],
        in_specs=[vmem, vmem],
        out_specs=[hbm, hbm],
        scratch_shapes=[pltpu.SemaphoreType.DMA((6,))],
        compiler_params=pltpu.CompilerParams(vmem_limit_bytes=1024 * 1024),
        cost_estimate=pl.CostEstimate(flops=0, bytes_accessed=36 * rows * columns, transcendentals=0),
        name="leave",
    )(*(pltpu.with_memory_space_constraint(value, pltpu.VMEM) for value in (velocity_next, inflow)))
    return velocity_next[:, None], inflow[None]


def solution(mesh):
    placed = (P(None, "gx", None, "yz"), P(), P(), P(), P(), P(), P(), P(), P("yz", None))
    return jax.shard_map(
        body,
        mesh=mesh,
        in_specs=placed,
        out_specs=(P(None, "gx", None, "yz"), P(None, None, None, "yz")),
        check_vma=False,
    )
```
